32 devices in a mesh: gx: 4 (over y, x), gy: 8 (over z, core).
Axes of the slice: x: 2, y: 2, z: 4, core: 2. Of those that a mesh axis runs over, the one named last changes fastest.
Arguments:
- potential: float32 [16, 256, 1024], P(None, 'gx', 'gy'), may hold values from -4 to 4
- labels: int32 [16, 256, 1024], P(None, 'gx', 'gy'), may hold values from 0 to 2, as said below
- voltages: float32 [2], replicated, may hold values from -3 to 3
- ion_blocks: bfloat16 [32, 32, 4096], P(('gx', 'gy')), may hold values from 0.19921875 to 2
- owner_map: int32 [32, 32], P(None, ('gx', 'gy')), may hold values from 0 to 31, as said below
Outputs:
- potential_next: float32 [16, 256, 1024], P(None, 'gx', 'gy')
The draws below stay inside these ranges and needn't reach their ends.
Inputs may be any that keep to these rules, and one draw needn't show every extreme that they name: `labels`: 0 marks plasma cells, 1 the screen electrode and 2 the accelerator electrode; the electrodes are plates of a few planes pierced by round apertures every 51 cells. For every brick k, the column owner_map[:, k] names each block index of brick k exactly once.
All inputs are finite; a program needn't handle non-finite values.
Results may differ from the reference program's by a relative error of at most 0.0003.
Values may be sent and summed in bfloat16 or wider, within the bound.
No kernel may reach another device: no remote copies, remote signals or barrier semaphores. Data moves between devices by JAX's collectives and lax.ppermute only.
A program may use at most 64 MiB of HBM per device.

```python
import jax
import jax.numpy as jnp
from jax import lax

NZ = 16
CX = 64
CY = 128
OV = 8
JACOBI = 4
SWEEPS = 3
PITCH = 51
BLOCKS = 32
TILE = 4096
NX = 256
NY = 1024
N_GX = 4
N_GY = 8


def draw_labels(key, part):
    subkeys = jax.random.split(key, 5)
    count_x = NX // PITCH + 1
    count_y = NY // PITCH + 1
    jitter_x = jax.random.randint(subkeys[0], (count_x, count_y), -3, 4)
    jitter_y = jax.random.randint(subkeys[1], (count_x, count_y), -3, 4)
    radius = jax.random.randint(subkeys[2], (count_x, count_y), PITCH // 4, PITCH * 2 // 5 + 1)
    x_index = jnp.arange(NX, dtype=jnp.int32)
    y_index = jnp.arange(NY, dtype=jnp.int32)
    cell_x = x_index // PITCH
    cell_y = y_index // PITCH
    table_x = jitter_x[cell_x[:, None], cell_y[None, :]]
    table_y = jitter_y[cell_x[:, None], cell_y[None, :]]
    table_radius = radius[cell_x[:, None], cell_y[None, :]]
    offset_x = x_index[:, None] - cell_x[:, None] * PITCH - PITCH // 2 - table_x
    offset_y = y_index[None, :] - cell_y[None, :] * PITCH - PITCH // 2 - table_y
    solid_cell = offset_x * offset_x + offset_y * offset_y > table_radius * table_radius
    thickness = max(1, NZ // 8)
    screen_start = jax.random.randint(subkeys[3], (), 0, NZ // 4 - thickness + 1)
    accel_start = jax.random.randint(subkeys[4], (), NZ // 2, NZ // 2 + NZ // 4 - thickness + 1)
    z_index = jnp.arange(NZ, dtype=jnp.int32)
    in_screen = (z_index >= screen_start) & (z_index < screen_start + thickness)
    in_accel = (z_index >= accel_start) & (z_index < accel_start + thickness)
    screen_cells = in_screen[:, None, None] & solid_cell[None, :, :]
    accel_cells = in_accel[:, None, None] & solid_cell[None, :, :]
    return jnp.where(screen_cells, 1, jnp.where(accel_cells, 2, 0)).astype(jnp.int32)


def draw_owner_map(key, part):
    scores = jax.random.randint(key, (BLOCKS, BLOCKS), 0, 1 << 20) * BLOCKS + lax.broadcasted_iota(jnp.int32, (BLOCKS, BLOCKS), 0)
    return jnp.argsort(scores, axis=0, stable=True).astype(jnp.int32)


def steps_of(own_key, shape, cuts, smallest, high):
    level = 1.0
    for dim, shards_of in cuts:
        draws = jax.random.uniform(jax.random.fold_in(jax.random.fold_in(own_key, 6), dim), (shards_of,), jnp.float32, smallest / len(cuts), high / len(cuts))
        level = level * jnp.repeat(jnp.exp(draws), shape[dim] // shards_of).reshape((-1,) + (1,) * (len(shape) - 1 - dim))
    return level


def scatter_about(stream_key, dims, width, reach, pieces=(), held_as=jnp.bfloat16):
    drawn = jax.random.normal(stream_key, dims, jnp.float32) * width
    if len(pieces) > 0:
        drawn = steps_of(stream_key, dims, pieces, -0.22, 0.18) * drawn
    return jnp.clip(drawn, min=-reach, max=reach).astype(held_as)


def setup_inputs(seed: int = 0) -> dict:
    streams_of = jax.random.split(jax.random.key(seed), 6)
    return {
        "potential": scatter_about(streams_of[0], (NZ, NX, NY), 1.0, 4.0, ((1, 4), (2, 8)), jnp.float32),
        "labels": draw_labels(jax.random.fold_in(streams_of[5], 71), 0),
        "voltages": jnp.clip(jax.random.uniform(streams_of[2], (2,), jnp.float32, -3.0, 3.0), -3.0, 3.0),
        "ion_blocks": jnp.clip(0.19921875 + 1.8007812 * jax.random.uniform(streams_of[3], (BLOCKS, BLOCKS, TILE), jnp.float32) ** steps_of(streams_of[3], (BLOCKS, BLOCKS, TILE), ((0, 32),), -0.2, 0.2), 0.19921875, 2.0).astype(jnp.bfloat16),
        "owner_map": draw_owner_map(jax.random.fold_in(streams_of[5], 71), 0),
    }


debye_term = 1.0
damping = 0.5


def neighbours(padded):
    center = padded[:, 1:-1, 1:-1]
    zero_plane = jnp.zeros_like(center[:1])
    summed = padded[:, 2:, 1:-1] + padded[:, :-2, 1:-1]
    summed = summed + padded[:, 1:-1, 2:] + padded[:, 1:-1, :-2]
    summed = summed + jnp.concatenate([center[1:], zero_plane], 0) + jnp.concatenate([zero_plane, center[:-1]], 0)
    return summed


def pad_plane(field, margin):
    return jnp.pad(field, ((0, 0), (margin, margin), (margin, margin)))


def local_solve(rhs_wide, coupling_wide):
    solution = jnp.zeros_like(rhs_wide)
    for iteration in range(JACOBI):
        solution = rhs_wide + coupling_wide * neighbours(pad_plane(solution, 1))
    return solution


def reference(potential, labels, voltages, ion_blocks, owner_map):
    def place(brick):
        return jnp.zeros((BLOCKS, TILE), jnp.bfloat16).at[owner_map[:, brick]].set(ion_blocks[:, brick])

    brick_blocks = lax.map(place, jnp.arange(BLOCKS, dtype=jnp.int32))
    charge = brick_blocks.reshape(N_GX, N_GY, NZ, CX, CY).transpose(2, 0, 3, 1, 4).reshape(NZ, NX, NY).astype(jnp.float32)
    plasma = labels == 0
    edge_value = jnp.where(labels == 1, voltages[0], voltages[1])
    growth = jnp.exp(potential)
    force = jnp.where(plasma, 6.0 * potential - neighbours(pad_plane(potential, 1)) - debye_term * (charge - growth), potential - edge_value)
    diagonal = jnp.where(plasma, 6.0 + debye_term * growth, 1.0)
    weight = -force / diagonal
    coupling = jnp.where(plasma, 1.0 / diagonal, 0.0)
    coupling_pad = pad_plane(coupling, OV)
    update = jnp.zeros_like(potential)
    for sweep_index in range(SWEEPS):
        if sweep_index == 0:
            scaled = weight
        else:
            scaled = weight - update + coupling * neighbours(pad_plane(update, 1))
        scaled_pad = pad_plane(scaled, OV)

        def add_brick(brick, summed):
            brick_x = (brick // N_GY).astype(jnp.int32)
            brick_y = (brick % N_GY).astype(jnp.int32)
            zero_index = jnp.zeros((), jnp.int32)
            start = (zero_index, brick_x * CX, brick_y * CY)
            extent = (NZ, CX + 2 * OV, CY + 2 * OV)
            rhs_wide = lax.dynamic_slice(scaled_pad, start, extent)
            coupling_wide = lax.dynamic_slice(coupling_pad, start, extent)
            part_solution = local_solve(rhs_wide, coupling_wide)
            current = lax.dynamic_slice(summed, start, extent)
            return lax.dynamic_update_slice(summed, current + part_solution, start)

        summed = lax.fori_loop(0, BLOCKS, add_brick, jnp.zeros((NZ, NX + 2 * OV, NY + 2 * OV), jnp.float32))
        update = update + damping * summed[:, OV:-OV, OV:-OV]
    return potential + update
```

```python
import functools

import jax
import jax.numpy as jnp
from jax import lax
from jax.experimental import pallas as pl
from jax.experimental.pallas import tpu as pltpu
from jax.sharding import PartitionSpec as P

HALO = 12
LOW = 32
HIGH = 64

debye_term = 1.0
damping = 0.5

f32 = jnp.float32
bf16 = jnp.bfloat16


def lane_iota(rows):
    return lax.broadcasted_iota(jnp.int32, (rows, 128), 1)


def between(lane, low, high):
    return (lane >= low) & (lane < high)


def roll(value, shift):
    shift = shift % 128
    return value if shift == 0 else pltpu.roll(value, shift, 1)


def x_pack_kernel(nz, rx, pot, lab, own_map, up, down):
    def row(ref, x):
        return ref[pl.ds(x, nz, stride=rx), :]

    for out, first, near in ((up, 0, 0), (down, rx - HALO, rx - 4)):
        for i in range(HALO):
            value = row(pot, first + i)
            high = value.astype(bf16)
            out[i] = high
            offset = first + i - near
            if 0 <= offset < 4:
                out[HALO + offset] = (value - high.astype(f32)).astype(bf16)
            out[HALO + 4 + i] = (row(lab, first + i) + 1).astype(f32).astype(bf16)
        out[2 * HALO + 4] = own_map[...].astype(bf16)


def y_pack_kernel(nz, rx, pot, lab, own_map, before, after, pa, la, left, right):
    wide = rx + 2 * HALO
    for i in range(HALO):
        value = before[i].astype(f32)
        if i >= HALO - 4:
            value = value + before[HALO + i - (HALO - 4)].astype(f32)
        pa[i] = value
        la[i] = before[HALO + 4 + i].astype(f32)
        value = after[i].astype(f32)
        if i < 4:
            value = value + after[HALO + i].astype(f32)
        pa[HALO + rx + i] = value
        la[HALO + rx + i] = after[HALO + 4 + i].astype(f32)

    def copy_rows(step, carry):
        for q in range(4):
            x = step * 4 + q
            pa[HALO + x] = pot[pl.ds(x, nz, stride=rx), :]
            la[HALO + x] = (lab[pl.ds(x, nz, stride=rx), :] + 1).astype(f32)
        return carry

    lax.fori_loop(0, rx // 4, copy_rows, 0)

    lane = lane_iota(nz)
    is_low = between(lane, 12, 16)
    is_label = lane >= 16
    group_of = lane // 32

    def group(g, carry):
        to_left = jnp.zeros((nz, 128), f32)
        to_right = jnp.zeros((nz, 128), f32)
        for q in range(4):
            value = pa[g * 4 + q]
            code = la[g * 4 + q]
            high = value.astype(bf16).astype(f32)
            low = value - high
            one = jnp.where(is_label, roll(code, 16), jnp.where(is_low, roll(low, 12), high))
            two = jnp.where(is_label, roll(code, 28), jnp.where(is_low, roll(low, 16), roll(high, 12)))
            here = group_of == q
            to_left = jnp.where(here, roll(one, 32 * q), to_left)
            to_right = jnp.where(here, roll(two, 32 * q), to_right)
        left[g] = to_left.astype(bf16)
        right[g] = to_right.astype(bf16)
        return carry

    lax.fori_loop(0, wide // 4, group, 0)
    row = lax.broadcasted_iota(jnp.int32, (nz, 128), 0)
    maps = jnp.where(
        row == 0,
        before[2 * HALO + 4].astype(f32),
        jnp.where(row == 1, own_map[...], after[2 * HALO + 4].astype(f32)),
    ).astype(bf16)
    left[wide // 4] = maps
    right[wide // 4] = maps


def neighbour_rows(ref_a, ref_b, i, nz, lane, low_row, high_row):
    a = ref_a[i, pl.ds(8, nz), :]
    b = ref_b[i, pl.ds(8, nz), :]
    first = lane == 0
    last = lane == 127
    ra, rb = roll(a, 1), roll(b, 1)
    la, lb = roll(a, 127), roll(b, 127)
    out_a = jnp.where(first, rb, ra) + jnp.where(last, lb, la)
    out_b = jnp.where(first, ra, rb) + jnp.where(last, la, lb)
    out_a = out_a + ref_a[i, pl.ds(7, nz), :] + ref_a[i, pl.ds(9, nz), :]
    out_b = out_b + ref_b[i, pl.ds(7, nz), :] + ref_b[i, pl.ds(9, nz), :]
    for beside in (low_row, high_row):
        if beside is not None:
            out_a = out_a + beside[0]
            out_b = out_b + beside[1]
    return out_a, out_b


def read_row(ref_a, ref_b, i, nz):
    return ref_a[i, pl.ds(8, nz), :], ref_b[i, pl.ds(8, nz), :]


def clear_pads(refs, count, nz):
    zero = jnp.zeros((8, 128), f32)

    def body(i, carry):
        for ref in refs:
            ref[i, pl.ds(0, 8), :] = zero
            ref[i, pl.ds(8 + nz, 8), :] = zero
        return carry

    lax.fori_loop(0, count, body, 0)


def spread(lane, left_right, a, q):
    base = roll(left_right, -32 * q)
    out = jnp.where(between(lane, 20, 32), roll(base, 20), jnp.zeros_like(base))
    out = jnp.where(between(lane, 119, 128), roll(base, 116), out)
    out = jnp.where(between(lane, 0, 9), roll(base, -16), out)
    out = jnp.where(between(lane, 64, 76), roll(base, 48), out)
    out = jnp.where(between(lane, 32, 41), roll(a, LOW), out)
    return jnp.where(between(lane, 55, 64), roll(a, HIGH), out)


def absent_lanes(lane):
    index = lax.axis_index("gy")
    none_before = between(lane, 20, 41) & (index == 0)
    none_after = between(lane, 55, 76) & (index == lax.axis_size("gy") - 1)
    return none_before | none_after


def weight_kernel(nz, rx, volts, pa, la, from_left, from_right, own_side, wa, wb, ca, cb, maps, ppa, ppb, lbb):
    wide = rx + 2 * HALO
    lane = lane_iota(nz)
    within = lane % 32
    clear_pads((ppa, ppb), wide, nz)

    def unpack(g, carry):
        tl = from_left[g].astype(f32)
        tr = from_right[g].astype(f32)
        pot_l = tl + jnp.where(between(within, 8, 12), roll(tl, -4), 0.0)
        pot_r = tr + jnp.where(within < 4, roll(tr, -12), 0.0)
        pot_lr = jnp.where(within < 12, pot_l, roll(pot_r, 16))
        lab_lr = jnp.where(within < 12, roll(tl, -16), tr)
        for q in range(4):
            i = g * 4 + q
            a = pa[i]
            ppa[i, pl.ds(8, nz), :] = a
            ppb[i, pl.ds(8, nz), :] = spread(lane, pot_lr, a, q)
            lbb[i] = spread(lane, lab_lr, la[i], q)
        return carry

    lax.fori_loop(0, wide // 4, unpack, 0)
    kept = between(lane, 0, 8) | between(lane, 21, 40) | between(lane, 56, 75) | between(lane, 120, 128)
    kept = kept & ~absent_lanes(lane)
    v0 = volts[0]
    v1 = volts[1]

    def rows(i, carry):
        n_a, n_b = neighbour_rows(
            ppa, ppb, i, nz, lane, read_row(ppa, ppb, i - 1, nz), read_row(ppa, ppb, i + 1, nz)
        )
        p_a, p_b = read_row(ppa, ppb, i, nz)
        for p, n, code, w_out, c_out, mask in (
            (p_a, n_a, la[i], wa, ca, None),
            (p_b, n_b, lbb[i], wb, cb, kept),
        ):
            growth = jnp.exp(p)
            inverse = 1.0 / (6.0 + debye_term * growth)
            plasma = between(code, 0.5, 1.5)
            edge = jnp.where(code < 2.5, v0, v1)
            inside = code > 0.5
            if mask is not None:
                plasma = plasma & mask
                inside = inside & mask
            w = jnp.where(plasma, (n - 6.0 * p - debye_term * growth) * inverse, edge - p)
            w_out[i] = jnp.where(inside, w, 0.0)
            c_out[i] = jnp.where(plasma, inverse, 0.0)
        return carry

    lax.fori_loop(1, wide - 1, rows, 0)
    zero = jnp.zeros((nz, 128), f32)
    for i in (0, wide - 1):
        for ref in (wa, wb, ca, cb):
            ref[i] = zero
    maps[pl.ds(0, 8), :] = from_left[wide // 4].astype(f32)[0:8].astype(jnp.int32)
    maps[pl.ds(8, 8), :] = own_side[wide // 4].astype(f32)[0:8].astype(jnp.int32)
    maps[pl.ds(16, 8), :] = from_right[wide // 4].astype(f32)[0:8].astype(jnp.int32)


def slot_kernel(count, ny, tiles, blocks, out, field):
    rows = tiles * 8
    for r in range(rows):
        field[pl.ds(r, count, stride=rows), :] = blocks[:, pl.ds(r * 128, 128)].astype(f32)
    lane = lane_iota(8)
    sub = lax.broadcasted_iota(jnp.int32, (8, 128), 0)

    def one(k, carry):
        def tile(offset, t):
            brick = lax.rem(k + offset + count, count)
            return field[pl.ds(pl.multiple_of(brick * rows + t * 8, 8), 8), :]

        parts = [tile(0, t) for t in range(tiles)]
        if tiles == 1:
            parts += [tile(ny, 0), tile(-ny, 0)]
        else:
            mixed = jnp.where(sub < 4, tile(ny, 1), tile(-ny, tiles - 2))
            parts += [tile(ny, 0), mixed, tile(-ny, tiles - 1)]

        def pair(offset, t, at):
            low = roll(tile(offset - 1, t), 12 + at)
            high = roll(tile(offset + 1, t), 16 + at)
            return jnp.where(between(lane, at, at + 12), low, high)

        sides = jnp.zeros((8, 128), f32)
        for t in range(tiles):
            sides = jnp.where(between(lane, 32 * t, 32 * t + 32), pair(0, t, 32 * t), sides)
        corners = jnp.where(lane < 32, pair(ny, 0, 0), pair(-ny, tiles - 1, 32))
        if tiles > 1:
            second = jnp.where(lane < 96, pair(ny, 1, 64), pair(-ny, tiles - 2, 96))
            corners = jnp.where(lane < 64, corners, second)
        parts += [sides, corners]
        out[k] = jnp.concatenate(parts, axis=0).astype(bf16)
        return carry

    lax.fori_loop(0, count, one, 0)


def sweep_kernel(nz, rx, count, tiles, maps, got, wa, wb, ca, cb, pot, out, *scratch):
    (ra, rb, xa, xb, ya, yb, ua, ub, cut_a, cut_b, ch_a, ch_l, ch_r, va, vb) = scratch
    wide = rx + 2 * HALO
    tall = rx + 32
    per_plane = rx // (8 * tiles)
    lane = lane_iota(nz)
    lane8 = lane_iota(8)
    clear_pads((ra, rb, xa, xb, ya, yb, ua, ub), wide, nz)
    clear_pads((cut_a, cut_b), cut_a.shape[0], nz)

    def place(p, carry):
        slot = got[p].astype(f32)
        pieces = [slot[8 * t : 8 * t + 8] for t in range(slot.shape[0] // 8)]

        def where_to(which, side):
            index = maps[which, p]
            z = index // per_plane
            part = index - z * per_plane
            if side == 0:
                return z, part, None
            depth = part if side > 0 else per_plane - 1 - part
            ok = depth * 8 * tiles < HALO
            return jnp.where(ok, z, nz), part, jnp.where(ok, depth, 0)

        def put(ref, z, row, value):
            ref[pl.ds(pl.multiple_of(z * tall + row, 8), 8), :] = value

        z, part, _ = where_to(9, 0)
        for t in range(tiles):
            put(ch_a, z, 16 + (part * tiles + t) * 8, pieces[t])
        zp, _, dp = where_to(10, 1)
        zm, _, dm = where_to(8, -1)
        if tiles == 1:
            put(ch_a, zp, 16 + rx + dp * 8, pieces[1])
            put(ch_a, zm, 8 - dm * 8, pieces[2])
            next_piece = 3
        else:
            put(ch_a, zp, 16 + rx, pieces[tiles])
            put(ch_a, zp, 24 + rx, pieces[tiles + 1])
            put(ch_a, zm, 0, pieces[tiles + 1])
            put(ch_a, zm, 8, pieces[tiles + 2])
            next_piece = tiles + 3
        sides = pieces[next_piece]
        corners = pieces[next_piece + 1]
        zl, part_l, _ = where_to(1, 0)
        zr, part_r, _ = where_to(17, 0)
        for t in range(tiles):
            value = roll(sides, -32 * t)
            put(ch_l, zl, 16 + (part_l * tiles + t) * 8, value)
            put(ch_r, zr, 16 + (part_r * tiles + t) * 8, value)
        for which, side, at, ref in ((2, 1, 0, ch_l), (18, 1, 0, ch_r), (0, -1, 32, ch_l), (16, -1, 32, ch_r)):
            z, _, depth = where_to(which, side)
            value = roll(corners, -at)
            if tiles == 1:
                put(ref, z, (16 + rx + depth * 8) if side > 0 else (8 - depth * 8), value)
            else:
                put(ref, z, (16 + rx) if side > 0 else 8, value)
                put(ref, z, (24 + rx) if side > 0 else 0, roll(corners, -at - 64))
        return carry

    lax.fori_loop(0, count, place, 0)

    def weights(i, carry):
        x = i + 4
        a = ch_a[pl.ds(x, nz, stride=tall), :]
        low = ch_l[pl.ds(x, nz, stride=tall), :]
        high = ch_r[pl.ds(x, nz, stride=tall), :]
        b = jnp.where(between(lane, 20, 32), roll(low, 20), 0.0)
        b = jnp.where(between(lane, 119, 128), roll(low, 116), b)
        b = jnp.where(between(lane, 0, 9), roll(high, -16), b)
        b = jnp.where(between(lane, 64, 76), roll(high, 48), b)
        b = jnp.where(between(lane, 32, 41), roll(a, LOW), b)
        b = jnp.where(between(lane, 55, 64), roll(a, HIGH), b)
        w_a = wa[i] + jnp.where(ca[i] > 0.0, debye_term * ca[i] * a, 0.0)
        w_b = wb[i] + jnp.where(cb[i] > 0.0, debye_term * cb[i] * b, 0.0)
        va[i] = w_a
        vb[i] = w_b
        ra[i, pl.ds(8, nz), :] = w_a
        rb[i, pl.ds(8, nz), :] = w_b
        return carry

    lax.fori_loop(1, wide - 1, weights, 0)

    def iterate(src, dst, low, high):
        def body(step, carry):
            i = low + step * 2
            rows = [read_row(*src, i + d, nz) for d in (-1, 0, 1, 2)]
            for d in (0, 1):
                n_a, n_b = neighbour_rows(*src, i + d, nz, lane, rows[d], rows[d + 2])
                dst[0][i + d, pl.ds(8, nz), :] = ra[i + d, pl.ds(8, nz), :] + ca[i + d] * n_a
                dst[1][i + d, pl.ds(8, nz), :] = rb[i + d, pl.ds(8, nz), :] + cb[i + d] * n_b
            return carry

        lax.fori_loop(0, (high - low) // 2, body, 0)

    def cut(level, at, edge, step):
        sources = {2: (ra, rb), 3: (xa, xb), 4: (ya, yb)}
        starts = {2: 0, 3: 1, 4: 3}
        whole = sources[level]
        for j in range(level - 1):
            i = edge + step * j
            if j < level - 2:
                own_refs, own_i = (cut_a, cut_b), at + starts[level - 1] + j
            else:
                own_refs, own_i = whole, i
            if j == 0:
                inner_out = None
            else:
                inner_out = read_row(cut_a, cut_b, at + starts[level - 1] + j - 1, nz)
            if j + 1 < level - 2:
                inner_in = read_row(cut_a, cut_b, at + starts[level - 1] + j + 1, nz)
            else:
                inner_in = read_row(*whole, i + step, nz)
            n_a, n_b = neighbour_rows(*own_refs, own_i, nz, lane, inner_out, inner_in)
            slot = at + starts[level] + j
            cut_a[slot, pl.ds(8, nz), :] = ra[i, pl.ds(8, nz), :] + ca[i] * n_a
            cut_b[slot, pl.ds(8, nz), :] = rb[i, pl.ds(8, nz), :] + cb[i] * n_b

    mid_low = HALO + 7
    mid_high = HALO + rx - 8
    end_low = HALO - 8
    end_high = HALO + rx + 7

    def combined(a, b):
        b_high = roll(b, HIGH)
        b_low = roll(b, -LOW)
        new_a = a + jnp.where(lane < 8, b_low, jnp.where(lane >= 120, b_high, 0.0))
        more = jnp.where(between(lane, 32, 41), roll(a, LOW), 0.0)
        more = jnp.where(between(lane, 55, 64), roll(a, HIGH), more)
        more = jnp.where((lane < 8) | between(lane, 64, 72), b_high, more)
        more = jnp.where(between(lane, 24, 32), roll(b, LOW), more)
        more = jnp.where(lane >= 120, b_low, more)
        return new_a, b + more

    ghost = (lane == 40) | (lane == 55) | absent_lanes(lane)
    index = lax.axis_index("gx")
    has_low = jnp.where(index > 0, 1.0, 0.0)
    has_high = jnp.where(index < lax.axis_size("gx") - 1, 1.0, 0.0)
    lowest = 1
    for sweep in range(3):
        last = sweep == 2
        if sweep > 0:
            lowest = lowest + 4

            def residual(step, carry):
                i = lowest + step * 2
                rows = [read_row(ua, ub, i + d, nz) for d in (-1, 0, 1, 2)]
                for d in (0, 1):
                    n_a, n_b = neighbour_rows(ua, ub, i + d, nz, lane, rows[d], rows[d + 2])
                    r_a = va[i + d] - rows[d + 1][0] + ca[i + d] * n_a
                    r_b = vb[i + d] - rows[d + 1][1] + cb[i + d] * n_b
                    ra[i + d, pl.ds(8, nz), :] = r_a
                    rb[i + d, pl.ds(8, nz), :] = jnp.where(ghost, 0.0, r_b)
                return carry

            lax.fori_loop(0, (wide - 2 * lowest) // 2, residual, 0)
        iterate((ra, rb), (xa, xb), lowest + 1, wide - lowest - 1)
        iterate((xa, xb), (ya, yb), lowest + 2, wide - lowest - 2)
        ends = [(0, mid_low, -1), (6, mid_high, 1)]
        if sweep == 0:
            ends += [(12, end_low, 1), (18, end_high, -1)]
        for at, edge, step in ends:
            for level in (2, 3, 4):
                cut(level, at, edge, step)
        low = lowest + 3
        iterate((ya, yb), (xa, xb), low, wide - low)

        def add(i, a, b):
            new_a, new_b = combined(a, b)
            if last:
                x = i - HALO
                total = ua[i, pl.ds(8, nz), :] + damping * new_a + pot[pl.ds(x, nz, stride=rx), :]
                out[pl.ds(x, nz, stride=rx), :] = total
                return
            new_a, new_b = damping * new_a, damping * new_b
            if sweep > 0:
                new_a = new_a + ua[i, pl.ds(8, nz), :]
                new_b = new_b + ub[i, pl.ds(8, nz), :]
            ua[i, pl.ds(8, nz), :] = new_a
            ub[i, pl.ds(8, nz), :] = new_b

        def span(first, end, factor):
            def body(i, carry):
                a, b = read_row(xa, xb, i, nz)
                if factor is not None:
                    a, b = a * factor, b * factor
                add(i, a, b)
                return carry

            lax.fori_loop(first, end, body, 0)

        first, end = low, wide - low
        if sweep == 0:
            for at, edge, step in ends[2:]:
                for j in range(3):
                    i = edge + step * j
                    a, b = read_row(xa, xb, i, nz)
                    c_a, c_b = read_row(cut_a, cut_b, at + 3 + j, nz)
                    add(i, a + c_a, b + c_b)
            first, end = low + 3, wide - low - 3
        span(first, mid_low - 2, 1.0 + has_low)
        span(mid_low + 1, mid_high, None)
        span(mid_high + 3, end, 1.0 + has_high)
        for (at, edge, step), has in zip(ends[:2], (has_low, has_high)):
            for j in range(3):
                i = edge + step * j
                a, b = read_row(xa, xb, i, nz)
                c_a, c_b = read_row(cut_a, cut_b, at + 3 + j, nz)
                add(i, a + has * c_a, b + has * c_b)


def vmem():
    return pl.BlockSpec(memory_space=pltpu.VMEM)


def smem():
    return pl.BlockSpec(memory_space=pltpu.SMEM)


def call(kernel, ins, outs, scratch=()):
    return pl.pallas_call(
        kernel,
        in_specs=ins,
        out_specs=jax.tree.map(lambda _: vmem(), outs),
        out_shape=outs,
        scratch_shapes=list(scratch),
        compiler_params=pltpu.CompilerParams(vmem_limit_bytes=50 << 20),
    )


def shifted(value, axis, steps):
    count = lax.axis_size(axis)
    first, last = max(0, -steps), min(count, count - steps)
    return lax.ppermute(value, axis, [(source, source + steps) for source in range(first, last)])


def on_device(potential, labels, voltages, ion_blocks, owner_map):
    nz, rx, ry = potential.shape
    wide = rx + 2 * HALO
    blocks = ion_blocks[0]
    count, cells = blocks.shape
    tiles = cells // (8 * ry)
    sds = jax.ShapeDtypeStruct
    pot = potential.reshape(nz * rx, ry)
    lab = labels.reshape(nz * rx, ry)
    ny = lax.axis_size("gy")

    slot_rows = 8 * (tiles + (2 if tiles == 1 else 3) + 2)
    slots = call(
        functools.partial(slot_kernel, count, ny, tiles),
        [vmem()],
        sds((count, slot_rows, ry), bf16),
        [pltpu.VMEM((count * tiles * 8, 128), f32)],
    )(blocks)
    got = lax.all_to_all(slots, ("gx", "gy"), split_axis=0, concat_axis=0, tiled=True)

    own_map = jnp.broadcast_to(
        jnp.pad(owner_map[:, 0].astype(f32), (0, 128 - count))[None], (nz, 128)
    )
    strip = sds((2 * HALO + 5, nz, ry), bf16)
    up, down = call(functools.partial(x_pack_kernel, nz, rx), [vmem()] * 3, (strip, strip))(
        pot, lab, own_map
    )
    before = shifted(down, "gx", 1)
    after = shifted(up, "gx", -1)
    field = sds((wide, nz, ry), f32)
    side = sds((wide // 4 + 1, nz, ry), bf16)
    pa, la, left, right = call(
        functools.partial(y_pack_kernel, nz, rx), [vmem()] * 5, (field, field, side, side)
    )(pot, lab, own_map, before, after)
    from_left = shifted(right, "gy", 1)
    from_right = shifted(left, "gy", -1)
    padded = pltpu.VMEM((wide, nz + 16, 128), f32)
    wa, wb, ca, cb, maps = call(
        functools.partial(weight_kernel, nz, rx),
        [smem()] + [vmem()] * 5,
        (field, field, field, field, sds((24, 128), jnp.int32)),
        [padded, padded, pltpu.VMEM((wide, nz, 128), f32)],
    )(voltages, pa, la, from_left, from_right, left)
    cuts = pltpu.VMEM((24, nz + 16, 128), f32)
    plane = pltpu.VMEM(((nz + 1) * (rx + 32), 128), f32)
    out = call(
        functools.partial(sweep_kernel, nz, rx, count, tiles),
        [smem()] + [vmem()] * 6,
        sds((nz * rx, ry), f32),
        [padded] * 8 + [cuts, cuts] + [plane] * 3 + [pltpu.VMEM((wide, nz, 128), f32)] * 2,
    )(maps, got, wa, wb, ca, cb, pot)
    return out.reshape(nz, rx, ry)


def solution(mesh):
    placed = (
        P(None, "gx", "gy"),
        P(None, "gx", "gy"),
        P(),
        P(("gx", "gy"), None, None),
        P(None, ("gx", "gy")),
    )
    return jax.shard_map(
        on_device, mesh=mesh, in_specs=placed, out_specs=P(None, "gx", "gy"), check_vma=False
    )
```

```python
import functools

import jax
import jax.numpy as jnp
from jax import lax
from jax.experimental import pallas as pl
from jax.experimental.pallas import tpu as pltpu
from jax.sharding import PartitionSpec as P

HALO = 12
debye_term = 1.0
damping = 0.5

f32 = jnp.float32
bf16 = jnp.bfloat16


def lane_iota(rows):
    return lax.broadcasted_iota(jnp.int32, (rows, 128), 1)


def between(lane, low, high):
    return (lane >= low) & (lane < high)


def roll(value, shift):
    shift = shift % 128
    return value if shift == 0 else pltpu.roll(value, shift, 1)


def x_pack_kernel(nz, rx, pot, lab, own_map, up, down):
    def row(ref, x):
        return ref[pl.ds(x, nz, stride=rx), :]

    for out, first, near in ((up, 0, 0), (down, rx - HALO, rx - 4)):
        for i in range(HALO):
            value = row(pot, first + i)
            high = value.astype(bf16)
            out[i] = high
            offset = first + i - near
            if 0 <= offset < 4:
                out[HALO + offset] = (value - high.astype(f32)).astype(bf16)
            out[HALO + 4 + i] = (row(lab, first + i) + 1).astype(f32).astype(bf16)
        out[2 * HALO + 4] = own_map[...].astype(bf16)


def y_pack_kernel(nz, rx, pot, lab, own_map, before, after, pa, la, left, right):
    wide = rx + 2 * HALO
    for i in range(HALO):
        value = before[i].astype(f32)
        if i >= HALO - 4:
            value = value + before[HALO + i - (HALO - 4)].astype(f32)
        pa[i] = value
        la[i] = before[HALO + 4 + i].astype(f32)
        value = after[i].astype(f32)
        if i < 4:
            value = value + after[HALO + i].astype(f32)
        pa[HALO + rx + i] = value
        la[HALO + rx + i] = after[HALO + 4 + i].astype(f32)

    def copy_rows(step, carry):
        for q in range(4):
            x = step * 4 + q
            pa[HALO + x] = pot[pl.ds(x, nz, stride=rx), :]
            la[HALO + x] = (lab[pl.ds(x, nz, stride=rx), :] + 1).astype(f32)
        return carry

    lax.fori_loop(0, rx // 4, copy_rows, 0)

    lane = lane_iota(nz)
    is_low = between(lane, 12, 16)
    is_label = lane >= 16
    group_of = lane // 32

    def group(g):
        to_left = jnp.zeros((nz, 128), f32)
        to_right = jnp.zeros((nz, 128), f32)
        for q in range(4):
            value = pa[g * 4 + q]
            code = la[g * 4 + q]
            high = value.astype(bf16).astype(f32)
            low = value - high
            one = jnp.where(is_label, roll(code, 16), jnp.where(is_low, roll(low, 12), high))
            two = jnp.where(is_label, roll(code, 28), jnp.where(is_low, roll(low, 16), roll(high, 12)))
            here = group_of == q
            to_left = jnp.where(here, roll(one, 32 * q), to_left)
            to_right = jnp.where(here, roll(two, 32 * q), to_right)
        left[g] = to_left.astype(bf16)
        right[g] = to_right.astype(bf16)

    def groups(first, size):
        for k in range(size):
            group(first + k)

    chunked(0, wide // 4, 4, groups)
    row = lax.broadcasted_iota(jnp.int32, (nz, 128), 0)
    maps = jnp.where(
        row == 0,
        before[2 * HALO + 4].astype(f32),
        jnp.where(row == 1, own_map[...], after[2 * HALO + 4].astype(f32)),
    ).astype(bf16)
    left[wide // 4] = maps
    right[wide // 4] = maps


NOWHERE = -1000


def place_of(column):
    return jnp.where(column < 128, 2 * column, 2 * column - 255)


def cell_of(place):
    cell = jnp.where(place <= 136, place, NOWHERE)
    cell = jnp.where(between(place, 148, 169), place - 160, cell)
    cell = jnp.where(between(place, 183, 204), place - 64, cell)
    return jnp.where(place >= 247, place - 256, cell)


def grid_of(rows, columns):
    return (
        lax.broadcasted_iota(jnp.int32, (rows, columns), 0),
        lax.broadcasted_iota(jnp.int32, (rows, columns), 1),
    )


def ones_where(condition):
    return jnp.where(condition, 1.0, 0.0).astype(bf16)


def parts_of(value):
    high = value.astype(bf16)
    rest = value - high.astype(f32)
    middle = rest.astype(bf16)
    return high, middle, (rest - middle.astype(f32)).astype(bf16)


def product(left, right):
    return jnp.dot(left, right, preferred_element_type=f32)


def read(ref, i, nz):
    return ref[i, pl.ds(8, nz), :]


def neighbour_rows(refs, i, nz, low_row, high_row):
    even, odd = read(refs[0], i, nz), read(refs[1], i, nz)
    out = [odd + roll(odd, 1), even + roll(even, 127)]
    for t in (0, 1):
        out[t] = out[t] + (refs[t][i, pl.ds(7, nz), :] + refs[t][i, pl.ds(9, nz), :])
        for beside in (low_row, high_row):
            if beside is not None:
                out[t] = out[t] + beside[t]
    return out


def read_row(refs, i, nz):
    return read(refs[0], i, nz), read(refs[1], i, nz)


def clear_pads(refs, count, nz):
    zero = jnp.zeros((count, 8, 128), f32)
    for ref in refs:
        ref[:, pl.ds(0, 8), :] = zero
        ref[:, pl.ds(8 + nz, 8), :] = zero


def chunked(low, high, most, fn):
    count = -(-(high - low) // most)
    size = -(-(high - low) // count)
    if count == 1:
        fn(low, size)
        return

    def body(step, carry):
        fn(jnp.minimum(low + step * size, high - size), size)
        return carry

    lax.fori_loop(0, count, body, 0)


def absent(place):
    index = lax.axis_index("gy")
    none_before = between(place, 148, 169) & (index == 0)
    none_after = between(place, 183, 204) & (index == lax.axis_size("gy") - 1)
    return none_before | none_after


def weight_kernel(nz, rx, volts, pa, la, from_left, from_right, own_side, we, wo, ce, co, maps, ppe, ppo, lbe, lbo):
    wide = rx + 2 * HALO
    groups = wide // 4
    clear_pads((ppe, ppo), wide, nz)
    row, column = grid_of(128, 256)
    cell = cell_of(place_of(column))
    own = ones_where(row == cell)
    row, column = grid_of(32, 256)
    cell = cell_of(place_of(column))
    low_side = cell < 0
    from_low, from_high = cell + HALO, cell - 128
    pot_low = ones_where(
        low_side & (((row < HALO) & (row == from_low)) | (between(row, 12, 16) & (row == from_low + 4)))
    )
    pot_high = ones_where(
        (cell >= 128) & (((row < HALO) & (row == from_high)) | (between(row, 12, 16) & (row == from_high + 12)))
    )
    lab_low = ones_where(low_side & between(row, 16, 28) & (row == from_low + 16))
    lab_high = ones_where((cell >= 128) & between(row, 16, 28) & (row == from_high + 16))

    def moved(matrix, q):
        pieces = [jnp.zeros((32, 256), bf16)] * 4
        pieces[q] = matrix
        return jnp.concatenate(pieces, axis=0)

    flat = (groups * nz, 128)
    left = from_left[pl.ds(0, groups)].reshape(flat)
    right = from_right[pl.ds(0, groups)].reshape(flat)
    for q in range(4):
        value = pa[pl.ds(q, groups, stride=4)].reshape(flat)
        high, middle, low = parts_of(value)
        pot = product(jnp.concatenate([high, left], axis=1), jnp.concatenate([own, moved(pot_low, q)], axis=0))
        pot = pot + product(
            jnp.concatenate([middle, right], axis=1), jnp.concatenate([own, moved(pot_high, q)], axis=0)
        )
        pot = (pot + product(low, own)).reshape(groups, nz, 256)
        ppe[pl.ds(q, groups, stride=4), pl.ds(8, nz), :] = pot[:, :, :128]
        ppo[pl.ds(q, groups, stride=4), pl.ds(8, nz), :] = pot[:, :, 128:]
        code = la[pl.ds(q, groups, stride=4)].reshape(flat).astype(bf16)
        lab = product(jnp.concatenate([code, left], axis=1), jnp.concatenate([own, moved(lab_low, q)], axis=0))
        lab = (lab + product(right, moved(lab_high, q))).reshape(groups, nz, 256)
        lbe[pl.ds(q, groups, stride=4)] = lab[:, :, :128]
        lbo[pl.ds(q, groups, stride=4)] = lab[:, :, 128:]
    lane = lane_iota(nz)
    kept = []
    for t in (0, 1):
        place = 2 * lane + t
        keep = (place < 136) | between(place, 149, 168) | between(place, 184, 203) | (place >= 248)
        kept.append(keep & ~absent(place))
    v0 = volts[0]
    v1 = volts[1]

    def rows(first, size):
        for k in range(size):
            i = first + k
            near = neighbour_rows((ppe, ppo), i, nz, read_row((ppe, ppo), i - 1, nz), read_row((ppe, ppo), i + 1, nz))
            for t, (p_ref, code_ref, w_out, c_out) in enumerate(((ppe, lbe, we, ce), (ppo, lbo, wo, co))):
                p = read(p_ref, i, nz)
                code = jnp.where(kept[t], code_ref[i], 0.0)
                growth = jnp.exp(p)
                inverse = 1.0 / (6.0 + debye_term * growth)
                plasma = between(code, 0.5, 1.5)
                edge = jnp.where(code < 2.5, v0, v1)
                w = jnp.where(plasma, (near[t] - 6.0 * p - debye_term * growth) * inverse, edge - p)
                w_out[i] = jnp.where(code > 0.5, w, 0.0)
                c_out[i] = jnp.where(plasma, inverse, 0.0)

    chunked(1, wide - 1, 22, rows)
    zero = jnp.zeros((nz, 128), f32)
    for i in (0, wide - 1):
        for ref in (we, wo, ce, co):
            ref[i] = zero
    for at, ref in ((0, from_left), (8, own_side), (16, from_right)):
        maps[pl.ds(at, 8), :] = ref[groups].astype(f32)[0:8].astype(jnp.int32)


def slot_kernel(count, ny, tiles, blocks, out, field):
    rows = tiles * 8
    for r in range(rows):
        field[pl.ds(r, count, stride=rows), :] = blocks[:, pl.ds(r * 128, 128)].astype(f32)
    lane = lane_iota(8)
    sub = lax.broadcasted_iota(jnp.int32, (8, 128), 0)

    def one(k, carry):
        def tile(offset, t):
            brick = lax.rem(k + offset + count, count)
            return field[pl.ds(pl.multiple_of(brick * rows + t * 8, 8), 8), :]

        parts = [tile(0, t) for t in range(tiles)]
        if tiles == 1:
            parts += [tile(ny, 0), tile(-ny, 0)]
        else:
            mixed = jnp.where(sub < 4, tile(ny, 1), tile(-ny, tiles - 2))
            parts += [tile(ny, 0), mixed, tile(-ny, tiles - 1)]

        def pair(offset, t, at):
            low = roll(tile(offset - 1, t), 12 + at)
            high = roll(tile(offset + 1, t), 16 + at)
            return jnp.where(between(lane, at, at + 12), low, high)

        sides = jnp.zeros((8, 128), f32)
        for t in range(tiles):
            sides = jnp.where(between(lane, 32 * t, 32 * t + 32), pair(0, t, 32 * t), sides)
        corners = jnp.where(lane < 32, pair(ny, 0, 0), pair(-ny, tiles - 1, 32))
        if tiles > 1:
            second = jnp.where(lane < 96, pair(ny, 1, 64), pair(-ny, tiles - 2, 96))
            corners = jnp.where(lane < 64, corners, second)
        parts += [sides, corners]
        out[k] = jnp.concatenate(parts, axis=0).astype(bf16)
        return carry

    def some(step, carry):
        for k in range(4):
            one(step * 4 + k, carry)
        return carry

    lax.fori_loop(0, count // 4, some, 0)


def sweep_kernel(nz, rx, count, tiles, maps, got, we, wo, ce, co, pot, out, *scratch):
    (re, ro, xe, xo, ye, yo, ue, uo, cut_e, cut_o, ch_a, ch_l, ch_r, ve, vo) = scratch
    rhs, xs, ys, us, cuts = (re, ro), (xe, xo), (ye, yo), (ue, uo), (cut_e, cut_o)
    weights, charged, couplings = (we, wo), (ve, vo), (ce, co)
    wide = rx + 2 * HALO
    tall = rx + 32
    per_plane = rx // (8 * tiles)
    lane = lane_iota(nz)
    index_x, index_y = lax.axis_index("gx"), lax.axis_index("gy")
    low_x, high_x = index_x > 0, index_x < lax.axis_size("gx") - 1
    has_low, has_high = jnp.where(low_x, 1.0, 0.0), jnp.where(high_x, 1.0, 0.0)
    clear_pads(rhs + xs + ys + us, wide, nz)
    clear_pads(cuts, cut_e.shape[0], nz)

    def place(p):
        slot = got[p].astype(f32)
        pieces = [slot[8 * t : 8 * t + 8] for t in range(slot.shape[0] // 8)]

        def where_to(which, side):
            index = maps[which, p]
            z = index // per_plane
            part = index - z * per_plane
            if side == 0:
                return z, part, None
            depth = part if side > 0 else per_plane - 1 - part
            ok = depth * 8 * tiles < HALO
            return jnp.where(ok, z, nz), part, jnp.where(ok, depth, 0)

        def put(ref, z, row, value):
            ref[pl.ds(pl.multiple_of(z * tall + row, 8), 8), :] = value

        z, part, _ = where_to(9, 0)
        for t in range(tiles):
            put(ch_a, z, 16 + (part * tiles + t) * 8, pieces[t])
        zp, _, dp = where_to(10, 1)
        zm, _, dm = where_to(8, -1)
        if tiles == 1:
            put(ch_a, zp, 16 + rx + dp * 8, pieces[1])
            put(ch_a, zm, 8 - dm * 8, pieces[2])
            next_piece = 3
        else:
            put(ch_a, zp, 16 + rx, pieces[tiles])
            put(ch_a, zp, 24 + rx, pieces[tiles + 1])
            put(ch_a, zm, 0, pieces[tiles + 1])
            put(ch_a, zm, 8, pieces[tiles + 2])
            next_piece = tiles + 3
        sides = pieces[next_piece]
        corners = pieces[next_piece + 1]
        zl, part_l, _ = where_to(1, 0)
        zr, part_r, _ = where_to(17, 0)
        for t in range(tiles):
            value = roll(sides, -32 * t)
            put(ch_l, zl, 16 + (part_l * tiles + t) * 8, value)
            put(ch_r, zr, 16 + (part_r * tiles + t) * 8, value)
        for at, side in ((0, 1), (32, -1)):
            value = roll(corners, -at)
            second = None if tiles == 1 else roll(corners, -at - 64)
            for which, ref in ((1 + side, ch_l), (17 + side, ch_r)):
                z, _, depth = where_to(which, side)
                if tiles == 1:
                    put(ref, z, (16 + rx + depth * 8) if side > 0 else (8 - depth * 8), value)
                else:
                    put(ref, z, (16 + rx) if side > 0 else 8, value)
                    put(ref, z, (24 + rx) if side > 0 else 0, second)

    def place_some(step, carry):
        for k in range(8):
            place(step * 8 + k)
        return carry

    lax.fori_loop(0, count // 8, place_some, 0)

    row, column = grid_of(256, 256)
    cell = cell_of(place_of(column))
    spread = ones_where(
        ((row < 128) & (row == cell))
        | (between(row, 128, 128 + HALO) & (row - (128 + HALO) == cell))
        | (between(row, 144, 144 + HALO) & (row - 16 == cell))
    )
    source = cell_of(place_of(row))
    gather = jnp.where((source == cell) & (cell != NOWHERE), damping, 0.0).astype(bf16)
    row, column = grid_of(256, 128)
    final = ones_where(cell_of(place_of(row)) == column)
    is_low = (lane < HALO) & (index_y > 0)
    is_high = between(lane, 16, 16 + HALO) & (index_y < lax.axis_size("gy") - 1)

    def add_charge(present):
        def rows(first, size):
            both = []
            for k in range(size):
                x = first + k + 4
                a = ch_a[pl.ds(x, nz, stride=tall), :]
                low = ch_l[pl.ds(x, nz, stride=tall), :]
                high = ch_r[pl.ds(x, nz, stride=tall), :]
                strip = jnp.where(is_low, low, jnp.where(is_high, high, 0.0))
                if present is not None:
                    a = jnp.where(present, a, 0.0)
                    strip = jnp.where(present, strip, 0.0)
                both.append(jnp.concatenate([a, strip], axis=1).astype(bf16))
            charge = product(jnp.concatenate(both, axis=0), spread)
            for k in range(size):
                i = first + k
                for t in (0, 1):
                    part = charge[k * nz : (k + 1) * nz, 128 * t : 128 * t + 128]
                    value = weights[t][i] + debye_term * couplings[t][i] * part
                    charged[t][i] = value
                    rhs[t][i, pl.ds(8, nz), :] = value

        return rows

    chunked(1, HALO, HALO, add_charge(low_x))
    chunked(HALO, HALO + rx, 16, add_charge(None))
    chunked(HALO + rx, wide - 1, HALO, add_charge(high_x))

    def iterate(src, dst, low, high):
        def rows(first, size):
            for k in range(size):
                i = first + k
                near = neighbour_rows(src, i, nz, read_row(src, i - 1, nz), read_row(src, i + 1, nz))
                for t in (0, 1):
                    dst[t][i, pl.ds(8, nz), :] = read(rhs[t], i, nz) + couplings[t][i] * near[t]

        chunked(low, high, 28, rows)

    def cut(level, at, edge, step):
        starts = {2: 0, 3: 1, 4: 3}
        whole = {2: rhs, 3: xs, 4: ys}[level]
        for j in range(level - 1):
            i = edge + step * j
            before = at + starts.get(level - 1, 0)
            changed = j < level - 2
            outer = None if j == 0 else read_row(cuts, before + j - 1, nz)
            inner = read_row(cuts, before + j + 1, nz) if j + 1 < level - 2 else read_row(whole, i + step, nz)
            near = neighbour_rows(cuts if changed else whole, before + j if changed else i, nz, outer, inner)
            for t in (0, 1):
                cuts[t][at + starts[level] + j, pl.ds(8, nz), :] = read(rhs[t], i, nz) + couplings[t][i] * near[t]

    ends = [(0, HALO + 7, -1), (6, HALO + rx - 8, 1), (12, HALO - 8, 1), (18, HALO + rx + 7, -1)]
    ghosts = [(2 * lane + t == 168) | (2 * lane + t == 183) | absent(2 * lane + t) for t in (0, 1)]
    own = lane < 64
    for sweep in range(3):
        last = sweep == 2
        lowest = 1 + 4 * sweep
        if sweep > 0:

            def residual(first, size):
                for k in range(size):
                    i = first + k
                    near = neighbour_rows(us, i, nz, read_row(us, i - 1, nz), read_row(us, i + 1, nz))
                    for t in (0, 1):
                        held = jnp.where(ghosts[t], 0.0, charged[t][i] - read(us[t], i, nz))
                        shared = jnp.where(ghosts[t], 0.0, near[t])
                        rhs[t][i, pl.ds(8, nz), :] = held + couplings[t][i] * shared

            chunked(lowest, wide - lowest, 28, residual)
        iterate(rhs, xs, lowest + 1, wide - lowest - 1)
        iterate(xs, ys, lowest + 2, wide - lowest - 2)
        some = ends if sweep == 0 else ends[:2]
        for level in (2, 3, 4):
            for at, edge, step in some:
                cut(level, at, edge, step)
        low, high = lowest + 3, wide - lowest - 3
        iterate(ys, xs, low, high)

        def scale(first, end, factor):
            for i in range(first, end):
                for t in (0, 1):
                    xs[t][i, pl.ds(8, nz), :] = read(xs[t], i, nz) * factor

        def add_cut(at, edge, step, factor, kept):
            for j in range(3):
                i = edge + step * j
                for t in (0, 1):
                    whole = read(xs[t], i, nz)
                    part = read(cuts[t], at + 3 + j, nz)
                    xs[t][i, pl.ds(8, nz), :] = (part + factor * whole) if kept else (whole + factor * part)

        mid_low, mid_high = HALO + 7, HALO + rx - 8
        if sweep == 0:
            add_cut(*ends[2], has_low, True)
            add_cut(*ends[3], has_high, True)
            scale(low + 3, mid_low - 2, 1.0 + has_low)
            scale(mid_high + 3, high - 3, 1.0 + has_high)
        else:
            scale(low, mid_low - 2, 1.0 + has_low)
            scale(mid_high + 3, high, 1.0 + has_high)
        add_cut(*ends[0], has_low, False)
        add_cut(*ends[1], has_high, False)

        def join(first, size):
            flat = (size * nz, 128)
            both = [xs[t][pl.ds(first, size), pl.ds(8, nz), :].reshape(flat) for t in (0, 1)]
            if last:
                keep = lane_iota(size * nz) < 64
                both = [
                    damping * both[t]
                    + jnp.where(keep, us[t][pl.ds(first, size), pl.ds(8, nz), :].reshape(flat), 0.0)
                    for t in (0, 1)
                ]
            parts = parts_of(jnp.concatenate(both, axis=1))
            matrix = final if last else gather
            total = product(parts[2], matrix) + product(parts[1], matrix) + product(parts[0], matrix)
            if last:
                for k in range(size):
                    x = first + k - HALO
                    out[pl.ds(x, nz, stride=rx), :] = total[k * nz : (k + 1) * nz] + pot[pl.ds(x, nz, stride=rx), :]
                return
            for t in (0, 1):
                value = total[:, 128 * t : 128 * t + 128].reshape(size, nz, 128)
                if sweep > 0:
                    value = value + us[t][pl.ds(first, size), pl.ds(8, nz), :]
                us[t][pl.ds(first, size), pl.ds(8, nz), :] = value

        for first in range(low, high, 16):
            join(first, min(16, high - first))


def vmem():
    return pl.BlockSpec(memory_space=pltpu.VMEM)


def smem():
    return pl.BlockSpec(memory_space=pltpu.SMEM)


def call(kernel, ins, outs, scratch=()):
    return pl.pallas_call(
        kernel,
        in_specs=ins,
        out_specs=jax.tree.map(lambda _: vmem(), outs),
        out_shape=outs,
        scratch_shapes=list(scratch),
        compiler_params=pltpu.CompilerParams(vmem_limit_bytes=50 << 20),
    )


def shifted(value, axis, steps):
    count = lax.axis_size(axis)
    first, last = max(0, -steps), min(count, count - steps)
    return lax.ppermute(value, axis, [(source, source + steps) for source in range(first, last)])


def on_device(potential, labels, voltages, ion_blocks, owner_map):
    nz, rx, ry = potential.shape
    wide = rx + 2 * HALO
    blocks = ion_blocks[0]
    count, cells = blocks.shape
    tiles = cells // (8 * ry)
    sds = jax.ShapeDtypeStruct
    pot = potential.reshape(nz * rx, ry)
    lab = labels.reshape(nz * rx, ry)
    ny = lax.axis_size("gy")

    slot_rows = 8 * (tiles + (2 if tiles == 1 else 3) + 2)
    slots = call(
        functools.partial(slot_kernel, count, ny, tiles),
        [vmem()],
        sds((count, slot_rows, ry), bf16),
        [pltpu.VMEM((count * tiles * 8, 128), f32)],
    )(blocks)
    got = lax.all_to_all(slots, ("gx", "gy"), split_axis=0, concat_axis=0, tiled=True)

    own_map = jnp.broadcast_to(
        jnp.pad(owner_map[:, 0].astype(f32), (0, 128 - count))[None], (nz, 128)
    )
    strip = sds((2 * HALO + 5, nz, ry), bf16)
    up, down = call(functools.partial(x_pack_kernel, nz, rx), [vmem()] * 3, (strip, strip))(
        pot, lab, own_map
    )
    before = shifted(down, "gx", 1)
    after = shifted(up, "gx", -1)
    field = sds((wide, nz, ry), f32)
    side = sds((wide // 4 + 1, nz, ry), bf16)
    pa, la, left, right = call(
        functools.partial(y_pack_kernel, nz, rx), [vmem()] * 5, (field, field, side, side)
    )(pot, lab, own_map, before, after)
    from_left = shifted(right, "gy", 1)
    from_right = shifted(left, "gy", -1)
    padded = pltpu.VMEM((wide, nz + 16, 128), f32)
    we, wo, ce, co, maps = call(
        functools.partial(weight_kernel, nz, rx),
        [smem()] + [vmem()] * 5,
        (field, field, field, field, sds((24, 128), jnp.int32)),
        [padded, padded] + [pltpu.VMEM((wide, nz, 128), f32)] * 2,
    )(voltages, pa, la, from_left, from_right, left)
    cuts = pltpu.VMEM((24, nz + 16, 128), f32)
    plane = pltpu.VMEM(((nz + 1) * (rx + 32), 128), f32)
    out = call(
        functools.partial(sweep_kernel, nz, rx, count, tiles),
        [smem()] + [vmem()] * 6,
        sds((nz * rx, ry), f32),
        [padded] * 8 + [cuts, cuts] + [plane] * 3 + [pltpu.VMEM((wide, nz, 128), f32)] * 2,
    )(maps, got, we, wo, ce, co, pot)
    return out.reshape(nz, rx, ry)


def solution(mesh):
    placed = (
        P(None, "gx", "gy"),
        P(None, "gx", "gy"),
        P(),
        P(("gx", "gy"), None, None),
        P(None, ("gx", "gy")),
    )
    return jax.shard_map(
        on_device, mesh=mesh, in_specs=placed, out_specs=P(None, "gx", "gy"), check_vma=False
    )
```

```python
import functools

import jax
import jax.numpy as jnp
from jax import lax
from jax.experimental import pallas as pl
from jax.experimental.pallas import tpu as pltpu
from jax.sharding import PartitionSpec as P

HALO = 12
JOIN = 20
TALL = 40
debye_term = 1.0
damping = 0.5

f32 = jnp.float32
bf16 = jnp.bfloat16


def lane_iota(rows):
    return lax.broadcasted_iota(jnp.int32, (rows, 128), 1)


def between(lane, low, high):
    return (lane >= low) & (lane < high)


def roll(value, shift):
    shift = shift % 128
    return value if shift == 0 else pltpu.roll(value, shift, 1)


def is_even(axis):
    return lax.rem(lax.axis_index(axis), 2) == 0


def chunked(low, high, most, fn):
    count = -(-(high - low) // most)
    size = -(-(high - low) // count)
    if count == 1:
        fn(low, size)
        return

    def body(step, carry):
        fn(jnp.minimum(low + step * size, high - size), size)
        return carry

    lax.fori_loop(0, count, body, 0)


def x_pack_kernel(nz, rx, pot, lab, own_map, one, two):
    even = is_even("gx")
    for out, is_last in ((one, even), (two, jnp.logical_not(even))):
        base = jnp.where(is_last, rx - HALO, 0)
        near = jnp.where(is_last, HALO - 4, 0)

        def row(ref, x):
            return ref[pl.ds(x, nz, stride=rx), :]

        for i in range(HALO):
            out[i] = row(pot, base + i).astype(bf16)
            out[HALO + 4 + i] = (row(lab, base + i) + 1).astype(f32).astype(bf16)
        for i in range(4):
            value = row(pot, base + near + i)
            out[HALO + i] = (value - value.astype(bf16).astype(f32)).astype(bf16)
        out[2 * HALO + 4] = own_map[pl.ds(0, nz), :].astype(bf16)


def strip_groups(nz, pa, la, one, two, first, size):
    lane = lane_iota(nz)
    is_low = between(lane, 12, 16)
    is_label = lane >= 16
    group_of = lane // 32
    even = is_even("gy")
    for g in range(size):
        to_left = jnp.zeros((nz, 128), f32)
        to_right = jnp.zeros((nz, 128), f32)
        for q in range(4):
            value = pa[(first + g) * 4 + q]
            code = la[(first + g) * 4 + q]
            high = value.astype(bf16).astype(f32)
            low = value - high
            left = jnp.where(is_label, roll(code, 16), jnp.where(is_low, roll(low, 12), high))
            right = jnp.where(is_label, roll(code, 28), jnp.where(is_low, roll(low, 16), roll(high, 12)))
            here = group_of == q
            to_left = jnp.where(here, roll(left, 32 * q), to_left)
            to_right = jnp.where(here, roll(right, 32 * q), to_right)
        one[first + g] = jnp.where(even, to_right, to_left).astype(bf16)
        two[first + g] = jnp.where(even, to_left, to_right).astype(bf16)


def y_own_kernel(nz, rx, pot, lab, pa, la, one, two):
    def copy_rows(first, size):
        for k in range(size):
            x = first + k
            pa[HALO + x] = pot[pl.ds(x, nz, stride=rx), :]
            la[HALO + x] = (lab[pl.ds(x, nz, stride=rx), :] + 1).astype(f32)

    chunked(0, rx, 16, copy_rows)
    chunked(
        HALO // 4, (HALO + rx) // 4, 4, lambda first, size: strip_groups(nz, pa, la, one, two, first, size)
    )


def y_edge_kernel(nz, rx, own_map, got_one, got_two, *refs):
    pa, la, one, two = refs[4:]
    wide = rx + 2 * HALO
    even = is_even("gx")

    def before(i):
        return jnp.where(even, got_two[i].astype(f32), got_one[i].astype(f32))

    def after(i):
        return jnp.where(even, got_one[i].astype(f32), got_two[i].astype(f32))

    for i in range(HALO):
        value = before(i)
        if i >= HALO - 4:
            value = value + before(HALO + i - (HALO - 4))
        pa[i] = value
        la[i] = before(HALO + 4 + i)
        value = after(i)
        if i < 4:
            value = value + after(HALO + i)
        pa[HALO + rx + i] = value
        la[HALO + rx + i] = after(HALO + 4 + i)
    strip_groups(nz, pa, la, one, two, 0, HALO // 4)
    strip_groups(nz, pa, la, one, two, (HALO + rx) // 4, HALO // 4)
    row = lax.broadcasted_iota(jnp.int32, (nz, 128), 0)
    last = 2 * HALO + 4
    maps = jnp.where(row == 0, before(last), jnp.where(row == 1, own_map[pl.ds(0, nz), :], after(last)))
    one[wide // 4] = maps.astype(bf16)
    two[wide // 4] = maps.astype(bf16)


NOWHERE = -1000


def place_of(column):
    return jnp.where(column < 128, 2 * column, 2 * column - 255)


def cell_of(place):
    cell = jnp.where(place <= 136, place, NOWHERE)
    cell = jnp.where(between(place, 148, 169), place - 160, cell)
    cell = jnp.where(between(place, 183, 204), place - 64, cell)
    return jnp.where(place >= 247, place - 256, cell)


def grid_of(rows, columns):
    return (
        lax.broadcasted_iota(jnp.int32, (rows, columns), 0),
        lax.broadcasted_iota(jnp.int32, (rows, columns), 1),
    )


def ones_where(condition):
    return jnp.where(condition, 1.0, 0.0).astype(bf16)


def parts_of(value):
    high = value.astype(bf16)
    rest = value - high.astype(f32)
    middle = rest.astype(bf16)
    return high, middle, (rest - middle.astype(f32)).astype(bf16)


def product(left, right):
    return jnp.dot(left, right, preferred_element_type=f32)


def read(ref, i, nz):
    return ref[i, pl.ds(8, nz), :]


def neighbour_rows(refs, i, nz, low_row, high_row):
    even, odd = read(refs[0], i, nz), read(refs[1], i, nz)
    out = [odd + roll(odd, 1), even + roll(even, 127)]
    for t in (0, 1):
        out[t] = out[t] + (refs[t][i, pl.ds(7, nz), :] + refs[t][i, pl.ds(9, nz), :])
        for beside in (low_row, high_row):
            if beside is not None:
                out[t] = out[t] + beside[t]
    return out


def read_row(refs, i, nz):
    return read(refs[0], i, nz), read(refs[1], i, nz)


def clear_pads(refs, count, nz):
    zero = jnp.zeros((count, 8, 128), f32)
    for ref in refs:
        ref[:, pl.ds(0, 8), :] = zero
        ref[:, pl.ds(8 + nz, 8), :] = zero


def absent(place):
    index = lax.axis_index("gy")
    none_before = between(place, 148, 169) & (index == 0)
    none_after = between(place, 183, 204) & (index == lax.axis_size("gy") - 1)
    return none_before | none_after


def weight_kernel(nz, rx, own_map, pa, la, got_one, got_two, own_side, wc, maps, ppe, ppo, lbe, lbo):
    we, wo, ce, co = (wc.at[k] for k in range(4))
    wide = rx + 2 * HALO
    groups = wide // 4
    clear_pads((ppe, ppo), wide, nz)
    row, column = grid_of(128, 256)
    cell = cell_of(place_of(column))
    own = ones_where(row == cell)
    row, column = grid_of(32, 256)
    cell = cell_of(place_of(column))
    low_side = cell < 0
    from_low, from_high = cell + HALO, cell - 128
    pot_low = ones_where(
        low_side & (((row < HALO) & (row == from_low)) | (between(row, 12, 16) & (row == from_low + 4)))
    )
    pot_high = ones_where(
        (cell >= 128) & (((row < HALO) & (row == from_high)) | (between(row, 12, 16) & (row == from_high + 12)))
    )
    lab_low = ones_where(low_side & between(row, 16, 28) & (row == from_low + 16))
    lab_high = ones_where((cell >= 128) & between(row, 16, 28) & (row == from_high + 16))

    def moved(matrix, q):
        pieces = [jnp.zeros((32, 256), bf16)] * 4
        pieces[q] = matrix
        return jnp.concatenate(pieces, axis=0)

    flat = (groups * nz, 128)
    even = is_even("gy")
    swapped_one = got_one[pl.ds(0, groups)].reshape(flat)
    swapped_two = got_two[pl.ds(0, groups)].reshape(flat)
    left = jnp.where(even, swapped_two, swapped_one)
    right = jnp.where(even, swapped_one, swapped_two)
    for q in range(4):
        value = pa[pl.ds(q, groups, stride=4)].reshape(flat)
        high, middle, low = parts_of(value)
        pot = product(jnp.concatenate([high, left], axis=1), jnp.concatenate([own, moved(pot_low, q)], axis=0))
        pot = pot + product(
            jnp.concatenate([middle, right], axis=1), jnp.concatenate([own, moved(pot_high, q)], axis=0)
        )
        pot = (pot + product(low, own)).reshape(groups, nz, 256)
        ppe[pl.ds(q, groups, stride=4), pl.ds(8, nz), :] = pot[:, :, :128]
        ppo[pl.ds(q, groups, stride=4), pl.ds(8, nz), :] = pot[:, :, 128:]
        code = la[pl.ds(q, groups, stride=4)].reshape(flat).astype(bf16)
        lab = product(jnp.concatenate([code, left], axis=1), jnp.concatenate([own, moved(lab_low, q)], axis=0))
        lab = (lab + product(right, moved(lab_high, q))).reshape(groups, nz, 256)
        lbe[pl.ds(q, groups, stride=4)] = lab[:, :, :128]
        lbo[pl.ds(q, groups, stride=4)] = lab[:, :, 128:]
    lane = lane_iota(nz)
    kept = []
    for t in (0, 1):
        place = 2 * lane + t
        keep = (place < 136) | between(place, 149, 168) | between(place, 184, 203) | (place >= 248)
        kept.append(keep & ~absent(place))
    v0 = jnp.broadcast_to(own_map[pl.ds(16, 1), :], (nz, 128))
    v1 = jnp.broadcast_to(own_map[pl.ds(17, 1), :], (nz, 128))

    def rows(first, size):
        for k in range(size):
            i = first + k
            near = neighbour_rows((ppe, ppo), i, nz, read_row((ppe, ppo), i - 1, nz), read_row((ppe, ppo), i + 1, nz))
            for t, (p_ref, code_ref, w_out, c_out) in enumerate(((ppe, lbe, we, ce), (ppo, lbo, wo, co))):
                p = read(p_ref, i, nz)
                code = jnp.where(kept[t], code_ref[i], 0.0)
                growth = jnp.exp(p)
                inverse = 1.0 / (6.0 + debye_term * growth)
                plasma = between(code, 0.5, 1.5)
                edge = jnp.where(code < 2.5, v0, v1)
                w = jnp.where(plasma, (near[t] - 6.0 * p - debye_term * growth) * inverse, edge - p)
                w_out[i] = jnp.where(code > 0.5, w, 0.0)
                c_out[i] = jnp.where(plasma, inverse, 0.0)

    chunked(1, wide - 1, 22, rows)
    zero = jnp.zeros((nz, 128), f32)
    for i in (0, wide - 1):
        for ref in (we, wo, ce, co):
            ref[i] = zero
    map_one, map_two = got_one[groups].astype(f32)[0:8], got_two[groups].astype(f32)[0:8]
    maps[pl.ds(0, 8), :] = jnp.where(even, map_two, map_one).astype(jnp.int32)
    maps[pl.ds(8, 8), :] = own_side[groups].astype(f32)[0:8].astype(jnp.int32)
    maps[pl.ds(16, 8), :] = jnp.where(even, map_one, map_two).astype(jnp.int32)


def slot_kernel(count, ny, tiles, blocks_in, owners_in, volts_in, pot_in, lab_in, slots, own, pot, lab, *scratch):
    field, blocks, out, owners, volts, in_sems, out_sems = scratch
    rows = tiles * 8
    pairs = [(owners_in, owners), (volts_in, volts), (pot_in, pot), (lab_in, lab)]
    copies = [pltpu.make_async_copy(*pair, in_sems.at[4 + k]) for k, pair in enumerate(pairs)]
    width = rows * 128 // 4
    columns = [pl.ds(k * width, width) for k in range(4)]
    block_copies = [
        pltpu.make_async_copy(blocks_in.at[:, part], blocks.at[:, part], in_sems.at[k]) for k, part in enumerate(columns)
    ]
    for copy in block_copies + copies:
        copy.start()
    own[...] = jnp.zeros(own.shape, f32)
    for r in range(rows):
        if r % (rows // 4) == 0:
            block_copies[r // (rows // 4)].wait()
        field[pl.ds(r, count, stride=rows), :] = blocks[:, pl.ds(r * 128, 128)].astype(f32)
    lane = lane_iota(8)
    sub = lax.broadcasted_iota(jnp.int32, (8, 128), 0)

    def one(k, carry):
        def tile(offset, t):
            brick = lax.rem(k + offset + count, count)
            return field[pl.ds(pl.multiple_of(brick * rows + t * 8, 8), 8), :]

        parts = [tile(0, t) for t in range(tiles)]
        if tiles == 1:
            parts += [tile(ny, 0), tile(-ny, 0)]
        else:
            mixed = jnp.where(sub < 4, tile(ny, 1), tile(-ny, tiles - 2))
            parts += [tile(ny, 0), mixed, tile(-ny, tiles - 1)]

        def pair(offset, t, at):
            low = roll(tile(offset - 1, t), 12 + at)
            high = roll(tile(offset + 1, t), 16 + at)
            return jnp.where(between(lane, at, at + 12), low, high)

        sides = jnp.zeros((8, 128), f32)
        for t in range(tiles):
            sides = jnp.where(between(lane, 32 * t, 32 * t + 32), pair(0, t, 32 * t), sides)
        corners = jnp.where(lane < 32, pair(ny, 0, 0), pair(-ny, tiles - 1, 32))
        if tiles > 1:
            second = jnp.where(lane < 96, pair(ny, 1, 64), pair(-ny, tiles - 2, 96))
            corners = jnp.where(lane < 64, corners, second)
        parts += [sides, corners]
        out[k] = jnp.concatenate(parts, axis=0).astype(bf16)
        return carry

    part = count // 4
    out_copies = []
    for step in range(4):
        chunked(step * part, (step + 1) * part, 8, lambda first, size: [one(first + k, 0) for k in range(size)])
        span = pl.ds(step * part, part)
        out_copies.append(pltpu.make_async_copy(out.at[span], slots.at[span], out_sems.at[step]))
        out_copies[-1].start()
    for copy in copies:
        copy.wait()
    own[pl.ds(0, 16), pl.ds(0, count)] = jnp.broadcast_to(owners[...].astype(f32), (16, count))
    for k in (0, 1):
        own[pl.ds(16 + k, 1), :] = jnp.full((1, 128), volts[k], f32)
    for copy in out_copies:
        copy.wait()


def sweep_kernel(nz, rx, count, tiles, maps_in, got, wc, pot, out, *scratch):
    (re, ro, xe, xo, ye, yo, ue, uo, cut_e, cut_o, ch_a, ch_s, ve, vo, maps, map_sem) = scratch
    map_copy = pltpu.make_async_copy(maps_in, maps, map_sem)
    map_copy.start()
    we, wo, ce, co = (wc.at[k] for k in range(4))
    rhs, xs, ys, us, cuts = (re, ro), (xe, xo), (ye, yo), (ue, uo), (cut_e, cut_o)
    weights, charged, couplings = (we, wo), (ve, vo), (ce, co)
    wide = rx + 2 * HALO
    tall = rx + TALL
    per_plane = rx // (8 * tiles)
    lane = lane_iota(nz)
    index_x, index_y = lax.axis_index("gx"), lax.axis_index("gy")
    low_x, high_x = index_x > 0, index_x < lax.axis_size("gx") - 1
    has_low, has_high = jnp.where(low_x, 1.0, 0.0), jnp.where(high_x, 1.0, 0.0)
    clear_pads(rhs + xs + ys + us, wide, nz)
    clear_pads(cuts, cut_e.shape[0], nz)

    low_lanes, high_lanes = lane_iota(8) < 16, lane_iota(8) >= 16

    def place(p):
        slot = got[p].astype(f32)
        pieces = [slot[8 * t : 8 * t + 8] for t in range(slot.shape[0] // 8)]

        def where_to(which, side):
            index = maps[which, p]
            z = index // per_plane
            part = index - z * per_plane
            if side == 0:
                return z, part, None
            depth = part if side > 0 else per_plane - 1 - part
            ok = depth * 8 * tiles < HALO
            return jnp.where(ok, z, nz), part, jnp.where(ok, depth, 0)

        def put(ref, z, row, value, mask=None):
            target = pl.ds(pl.multiple_of(z * tall + row, 8), 8)
            if mask is None:
                ref[target, :] = value
            else:
                pltpu.store(ref.at[target, :], value, mask=mask)

        z, part, _ = where_to(9, 0)
        for t in range(tiles):
            put(ch_a, z, 16 + (part * tiles + t) * 8, pieces[t])
        zp, _, dp = where_to(10, 1)
        zm, _, dm = where_to(8, -1)
        if tiles == 1:
            put(ch_a, zp, 16 + rx + dp * 8, pieces[1])
            put(ch_a, zm, 8 - dm * 8, pieces[2])
            next_piece = 3
        else:
            put(ch_a, zp, 16 + rx, pieces[tiles])
            put(ch_a, zp, 24 + rx, pieces[tiles + 1])
            put(ch_a, zm, 0, pieces[tiles + 1])
            put(ch_a, zm, 8, pieces[tiles + 2])
            next_piece = tiles + 3
        sides = pieces[next_piece]
        corners = pieces[next_piece + 1]
        zl, part_l, _ = where_to(1, 0)
        zr, part_r, _ = where_to(17, 0)
        for t in range(tiles):
            value = roll(sides, -32 * t)
            put(ch_s, zl, 16 + (part_l * tiles + t) * 8, value, low_lanes)
            put(ch_s, zr, 16 + (part_r * tiles + t) * 8, value, high_lanes)
        for at, side in ((0, 1), (32, -1)):
            value = roll(corners, -at)
            second = None if tiles == 1 else roll(corners, -at - 64)
            for which, lanes in ((1 + side, low_lanes), (17 + side, high_lanes)):
                z, _, depth = where_to(which, side)
                if tiles == 1:
                    put(ch_s, z, (16 + rx + depth * 8) if side > 0 else (8 - depth * 8), value, lanes)
                else:
                    put(ch_s, z, (16 + rx) if side > 0 else 8, value, lanes)
                    put(ch_s, z, (24 + rx) if side > 0 else 0, second, lanes)

    row, column = grid_of(256, 256)
    cell = cell_of(place_of(column))
    spread = ones_where(
        ((row < 128) & (row == cell))
        | (between(row, 128, 128 + HALO) & (row - (128 + HALO) == cell))
        | (between(row, 144, 144 + HALO) & (row - 16 == cell))
    )
    source = cell_of(place_of(row))
    gather = jnp.where((source == cell) & (cell != NOWHERE), damping, 0.0).astype(bf16)
    row, column = grid_of(256, 128)
    final = ones_where(cell_of(place_of(row)) == column)
    is_strip = (lane < HALO) & (index_y > 0)
    is_strip = is_strip | (between(lane, 16, 16 + HALO) & (index_y < lax.axis_size("gy") - 1))

    map_copy.wait()
    chunked(0, count, 8, lambda first, size: [place(first + p) for p in range(size)])

    def add_charge(present):
        def rows(first, size):
            both = []
            for k in range(size):
                x = first + k + 4
                a = ch_a[pl.ds(x, nz, stride=tall), :]
                strip = jnp.where(is_strip, ch_s[pl.ds(x, nz, stride=tall), :], 0.0)
                if present is not None:
                    a = jnp.where(present, a, 0.0)
                    strip = jnp.where(present, strip, 0.0)
                both.append(jnp.concatenate([a, strip], axis=1).astype(bf16))
            charge = product(jnp.concatenate(both, axis=0), spread)
            for k in range(size):
                i = first + k
                for t in (0, 1):
                    part = charge[k * nz : (k + 1) * nz, 128 * t : 128 * t + 128]
                    value = weights[t][i] + debye_term * couplings[t][i] * part
                    charged[t][i] = value
                    rhs[t][i, pl.ds(8, nz), :] = value

        return rows

    chunked(1, HALO, HALO, add_charge(low_x))
    chunked(HALO, HALO + rx, 32, add_charge(None))
    chunked(HALO + rx, wide - 1, HALO, add_charge(high_x))

    def iterate(src, dst, low, high):
        def rows(first, size):
            for k in range(size):
                i = first + k
                near = neighbour_rows(src, i, nz, read_row(src, i - 1, nz), read_row(src, i + 1, nz))
                for t in (0, 1):
                    dst[t][i, pl.ds(8, nz), :] = read(rhs[t], i, nz) + couplings[t][i] * near[t]

        chunked(low, high, 42, rows)

    def cut(level, at, edge, step):
        starts = {2: 0, 3: 1, 4: 3}
        whole = {2: rhs, 3: xs, 4: ys}[level]
        for j in range(level - 1):
            i = edge + step * j
            before = at + starts.get(level - 1, 0)
            changed = j < level - 2
            outer = None if j == 0 else read_row(cuts, before + j - 1, nz)
            inner = read_row(cuts, before + j + 1, nz) if j + 1 < level - 2 else read_row(whole, i + step, nz)
            near = neighbour_rows(cuts if changed else whole, before + j if changed else i, nz, outer, inner)
            for t in (0, 1):
                cuts[t][at + starts[level] + j, pl.ds(8, nz), :] = read(rhs[t], i, nz) + couplings[t][i] * near[t]

    ends = [(0, HALO + 7, -1), (6, HALO + rx - 8, 1), (12, HALO - 8, 1), (18, HALO + rx + 7, -1)]
    ghosts = [(2 * lane + t == 168) | (2 * lane + t == 183) | absent(2 * lane + t) for t in (0, 1)]
    own = lane < 64
    for sweep in range(3):
        last = sweep == 2
        lowest = 1 + 4 * sweep
        if sweep > 0:

            def residual(first, size):
                for k in range(size):
                    i = first + k
                    near = neighbour_rows(us, i, nz, read_row(us, i - 1, nz), read_row(us, i + 1, nz))
                    for t in (0, 1):
                        held = jnp.where(ghosts[t], 0.0, charged[t][i] - read(us[t], i, nz))
                        shared = jnp.where(ghosts[t], 0.0, near[t])
                        rhs[t][i, pl.ds(8, nz), :] = held + couplings[t][i] * shared

            chunked(lowest, wide - lowest, 42, residual)
        iterate(rhs, xs, lowest + 1, wide - lowest - 1)
        iterate(xs, ys, lowest + 2, wide - lowest - 2)
        some = ends if sweep == 0 else ends[:2]
        for level in (2, 3, 4):
            for at, edge, step in some:
                cut(level, at, edge, step)
        low, high = lowest + 3, wide - lowest - 3
        iterate(ys, xs, low, high)

        def scale(first, end, factor):
            for i in range(first, end):
                for t in (0, 1):
                    xs[t][i, pl.ds(8, nz), :] = read(xs[t], i, nz) * factor

        def add_cut(at, edge, step, factor, kept):
            for j in range(3):
                i = edge + step * j
                for t in (0, 1):
                    whole = read(xs[t], i, nz)
                    part = read(cuts[t], at + 3 + j, nz)
                    xs[t][i, pl.ds(8, nz), :] = (part + factor * whole) if kept else (whole + factor * part)

        mid_low, mid_high = HALO + 7, HALO + rx - 8
        if sweep == 0:
            add_cut(*ends[2], has_low, True)
            add_cut(*ends[3], has_high, True)
            scale(low + 3, mid_low - 2, 1.0 + has_low)
            scale(mid_high + 3, high - 3, 1.0 + has_high)
        else:
            scale(low, mid_low - 2, 1.0 + has_low)
            scale(mid_high + 3, high, 1.0 + has_high)
        add_cut(*ends[0], has_low, False)
        add_cut(*ends[1], has_high, False)

        def join(first, size):
            flat = (size * nz, 128)
            both = [xs[t][pl.ds(first, size), pl.ds(8, nz), :].reshape(flat) for t in (0, 1)]
            if last:
                keep = lane_iota(size * nz) < 64
                both = [
                    damping * both[t]
                    + jnp.where(keep, us[t][pl.ds(first, size), pl.ds(8, nz), :].reshape(flat), 0.0)
                    for t in (0, 1)
                ]
            whole = jnp.concatenate(both, axis=1)
            high = whole.astype(bf16)
            rest = (whole - high.astype(f32)).astype(bf16)
            matrix = final if last else gather
            total = product(rest, matrix) + product(high, matrix)
            if last:
                for k in range(size):
                    x = first + k - HALO
                    out[pl.ds(x, nz, stride=rx), :] = total[k * nz : (k + 1) * nz] + pot[pl.ds(x, nz, stride=rx), :]
                return
            for t in (0, 1):
                value = total[:, 128 * t : 128 * t + 128].reshape(size, nz, 128)
                if sweep > 0:
                    value = value + us[t][pl.ds(first, size), pl.ds(8, nz), :]
                us[t][pl.ds(first, size), pl.ds(8, nz), :] = value

        for first in range(low, high, JOIN):
            join(first, min(JOIN, high - first))


def vmem():
    return pl.BlockSpec(memory_space=pltpu.VMEM)


def smem():
    return pl.BlockSpec(memory_space=pltpu.SMEM)


def hbm():
    return pl.BlockSpec(memory_space=pltpu.HBM)


def anywhere():
    return pl.BlockSpec(memory_space=pl.ANY)


def call(kernel, ins, outs, scratch=(), aliases=(), room=8):
    return pl.pallas_call(
        kernel,
        in_specs=ins,
        out_specs=jax.tree.map(lambda _: vmem(), outs),
        out_shape=outs,
        scratch_shapes=list(scratch),
        input_output_aliases=dict(aliases),
        compiler_params=pltpu.CompilerParams(vmem_limit_bytes=room << 20),
    )


def swapped(value, axis, first):
    pairs = []
    for low in range(first, lax.axis_size(axis) - 1, 2):
        pairs += [(low, low + 1), (low + 1, low)]
    return lax.ppermute(value, axis, pairs)


def on_device(potential, labels, voltages, ion_blocks, owner_map):
    nz, rx, ry = potential.shape
    wide = rx + 2 * HALO
    blocks = ion_blocks[0]
    count, cells = blocks.shape
    tiles = cells // (8 * ry)
    sds = jax.ShapeDtypeStruct
    ny = lax.axis_size("gy")

    slot_rows = 8 * (tiles + (2 if tiles == 1 else 3) + 2)
    slot_shape = (count, slot_rows, ry)
    brick = (nz, rx, ry)
    slots, own_map, potential, labels = pl.pallas_call(
        functools.partial(slot_kernel, count, ny, tiles),
        in_specs=[hbm()] * 5,
        out_specs=(hbm(), vmem(), vmem(), vmem()),
        out_shape=(sds(slot_shape, bf16), sds((24, ry), f32), sds(brick, f32), sds(brick, jnp.int32)),
        scratch_shapes=[
            pltpu.VMEM((count * tiles * 8, 128), f32),
            pltpu.VMEM((count, cells), bf16),
            pltpu.VMEM(slot_shape, bf16),
            pltpu.VMEM((1, count), jnp.int32),
            pltpu.SMEM((2,), f32),
            pltpu.SemaphoreType.DMA((8,)),
            pltpu.SemaphoreType.DMA((4,)),
        ],
        compiler_params=pltpu.CompilerParams(vmem_limit_bytes=12 << 20),
    )(*(pltpu.with_memory_space_constraint(v, pltpu.HBM) for v in (blocks, owner_map.reshape(1, count), voltages, potential, labels)))
    pot = potential.reshape(nz * rx, ry)
    lab = labels.reshape(nz * rx, ry)

    strip = sds((2 * HALO + 5, nz, ry), bf16)
    one, two = call(
        functools.partial(x_pack_kernel, nz, rx),
        [vmem()] * 3,
        (strip, strip),
    )(pot, lab, own_map)
    one = swapped(one, "gx", 0)
    two = swapped(two, "gx", 1)

    got = lax.all_to_all(slots, ("gx", "gy"), split_axis=0, concat_axis=0, tiled=True)

    field = sds((wide, nz, ry), f32)
    side = sds((wide // 4 + 1, nz, ry), bf16)
    packed = (field, field, side, side)
    pa, la, left, right = call(functools.partial(y_own_kernel, nz, rx), [vmem()] * 2, packed)(pot, lab)
    pa, la, left, right = call(
        functools.partial(y_edge_kernel, nz, rx), [vmem()] * 7, packed, (), {3: 0, 4: 1, 5: 2, 6: 3}
    )(own_map, one, two, pa, la, left, right)
    got_one = swapped(left, "gy", 0)
    got_two = swapped(right, "gy", 1)
    padded = pltpu.VMEM((wide, nz + 16, 128), f32)
    wc, maps = call(
        functools.partial(weight_kernel, nz, rx),
        [vmem()] * 6,
        (sds((4, wide, nz, ry), f32), sds((24, 128), jnp.int32)),
        [padded, padded]
        + [pltpu.VMEM((wide, nz, 128), f32)] * 2,
        room=16,
    )(own_map, pa, la, got_one, got_two, left)
    cuts = pltpu.VMEM((24, nz + 16, 128), f32)
    plane = pltpu.VMEM(((nz + 1) * (rx + TALL), 128), f32)
    out = call(
        functools.partial(sweep_kernel, nz, rx, count, tiles),
        [anywhere()] + [vmem()] * 3,
        sds((nz * rx, ry), f32),
        [padded] * 8
        + [cuts, cuts]
        + [plane] * 2
        + [pltpu.VMEM((wide, nz, 128), f32)] * 2
        + [
            pltpu.SMEM((24, 128), jnp.int32),
            pltpu.SemaphoreType.DMA,
        ],
        room=20,
    )(maps, got, wc, pot)
    return out.reshape(nz, rx, ry)


def solution(mesh):
    placed = (
        P(None, "gx", "gy"),
        P(None, "gx", "gy"),
        P(),
        P(("gx", "gy"), None, None),
        P(None, ("gx", "gy")),
    )
    return jax.shard_map(
        on_device, mesh=mesh, in_specs=placed, out_specs=P(None, "gx", "gy"), check_vma=False
    )
```

```python
import functools

import jax
import jax.numpy as jnp
from jax import lax
from jax.experimental import pallas as pl
from jax.experimental.pallas import tpu as pltpu
from jax.sharding import PartitionSpec as P

HALO = 12
JOIN = 40
TALL = 40
debye_term = 1.0
damping = 0.5

f32 = jnp.float32
bf16 = jnp.bfloat16


def lane_iota(rows):
    return lax.broadcasted_iota(jnp.int32, (rows, 128), 1)


def between(lane, low, high):
    return (lane >= low) & (lane < high)


def roll(value, shift):
    shift = shift % 128
    return value if shift == 0 else pltpu.roll(value, shift, 1)


def is_even(axis):
    return lax.rem(lax.axis_index(axis), 2) == 0


def chunked(low, high, most, fn):
    count = -(-(high - low) // most)
    size = -(-(high - low) // count)
    if count == 1:
        fn(low, size)
        return

    def body(step, carry):
        fn(jnp.minimum(low + step * size, high - size), size)
        return carry

    lax.fori_loop(0, count, body, 0)


def x_pack_kernel(nz, rx, pot, lab, own_map, one, two):
    even = is_even("gx")
    for out, is_last in ((one, even), (two, jnp.logical_not(even))):
        base = jnp.where(is_last, rx - HALO, 0)
        near = jnp.where(is_last, HALO - 4, 0)

        def row(ref, x):
            return ref[pl.ds(x, nz, stride=rx), :]

        for i in range(HALO):
            out[i] = row(pot, base + i).astype(bf16)
            out[HALO + 4 + i] = (row(lab, base + i) + 1).astype(f32).astype(bf16)
        for i in range(4):
            value = row(pot, base + near + i)
            out[HALO + i] = (value - value.astype(bf16).astype(f32)).astype(bf16)
        out[2 * HALO + 4] = own_map[pl.ds(0, nz), :].astype(bf16)


def strip_groups(nz, pa, la, one, two, first, size):
    lane = lane_iota(nz)
    is_low = between(lane, 12, 16)
    is_label = lane >= 16
    group_of = lane // 32
    even = is_even("gy")
    for g in range(size):
        to_left = jnp.zeros((nz, 128), f32)
        to_right = jnp.zeros((nz, 128), f32)
        for q in range(4):
            value = pa[(first + g) * 4 + q]
            code = la[(first + g) * 4 + q]
            high = value.astype(bf16).astype(f32)
            low = value - high
            left = jnp.where(is_label, roll(code, 16), jnp.where(is_low, roll(low, 12), high))
            right = jnp.where(is_label, roll(code, 28), jnp.where(is_low, roll(low, 16), roll(high, 12)))
            here = group_of == q
            to_left = jnp.where(here, roll(left, 32 * q), to_left)
            to_right = jnp.where(here, roll(right, 32 * q), to_right)
        one[first + g] = jnp.where(even, to_right, to_left).astype(bf16)
        two[first + g] = jnp.where(even, to_left, to_right).astype(bf16)


def y_own_kernel(nz, rx, pot, lab, pa, la, one, two):
    def copy_rows(first, size):
        for k in range(size):
            x = first + k
            pa[HALO + x] = pot[pl.ds(x, nz, stride=rx), :]
            la[HALO + x] = (lab[pl.ds(x, nz, stride=rx), :] + 1).astype(f32)

    chunked(0, rx, 64, copy_rows)
    chunked(
        HALO // 4, (HALO + rx) // 4, 4, lambda first, size: strip_groups(nz, pa, la, one, two, first, size)
    )


def y_edge_kernel(nz, rx, own_map, got_one, got_two, *refs):
    pa, la, one, two = refs[4:]
    wide = rx + 2 * HALO
    even = is_even("gx")

    def before(i):
        return jnp.where(even, got_two[i].astype(f32), got_one[i].astype(f32))

    def after(i):
        return jnp.where(even, got_one[i].astype(f32), got_two[i].astype(f32))

    for i in range(HALO):
        value = before(i)
        if i >= HALO - 4:
            value = value + before(HALO + i - (HALO - 4))
        pa[i] = value
        la[i] = before(HALO + 4 + i)
        value = after(i)
        if i < 4:
            value = value + after(HALO + i)
        pa[HALO + rx + i] = value
        la[HALO + rx + i] = after(HALO + 4 + i)
    strip_groups(nz, pa, la, one, two, 0, HALO // 4)
    strip_groups(nz, pa, la, one, two, (HALO + rx) // 4, HALO // 4)
    row = lax.broadcasted_iota(jnp.int32, (nz, 128), 0)
    last = 2 * HALO + 4
    maps = jnp.where(row == 0, before(last), jnp.where(row == 1, own_map[pl.ds(0, nz), :], after(last)))
    one[wide // 4] = maps.astype(bf16)
    two[wide // 4] = maps.astype(bf16)


NOWHERE = -1000


def place_of(column):
    return jnp.where(column < 128, 2 * column, 2 * column - 255)


def cell_of(place):
    cell = jnp.where(place <= 136, place, NOWHERE)
    cell = jnp.where(between(place, 148, 169), place - 160, cell)
    cell = jnp.where(between(place, 183, 204), place - 64, cell)
    return jnp.where(place >= 247, place - 256, cell)


def grid_of(rows, columns):
    return (
        lax.broadcasted_iota(jnp.int32, (rows, columns), 0),
        lax.broadcasted_iota(jnp.int32, (rows, columns), 1),
    )


def ones_where(condition):
    return jnp.where(condition, 1.0, 0.0).astype(bf16)


def parts_of(value):
    high = value.astype(bf16)
    rest = value - high.astype(f32)
    middle = rest.astype(bf16)
    return high, middle, (rest - middle.astype(f32)).astype(bf16)


def product(left, right):
    return jnp.dot(left, right, preferred_element_type=f32)


def read(ref, i, nz):
    return ref[i, pl.ds(8, nz), :]


def neighbour_rows(refs, i, nz, low_row, high_row):
    even, odd = read(refs[0], i, nz), read(refs[1], i, nz)
    out = [odd + roll(odd, 1), even + roll(even, 127)]
    for t in (0, 1):
        out[t] = out[t] + (refs[t][i, pl.ds(7, nz), :] + refs[t][i, pl.ds(9, nz), :])
        for beside in (low_row, high_row):
            if beside is not None:
                out[t] = out[t] + beside[t]
    return out


def read_row(refs, i, nz):
    return read(refs[0], i, nz), read(refs[1], i, nz)


def clear_pads(refs, count, nz):
    zero = jnp.zeros((count, 8, 128), f32)
    for ref in refs:
        ref[:, pl.ds(0, 8), :] = zero
        ref[:, pl.ds(8 + nz, 8), :] = zero


def absent(place):
    index = lax.axis_index("gy")
    none_before = between(place, 148, 169) & (index == 0)
    none_after = between(place, 183, 204) & (index == lax.axis_size("gy") - 1)
    return none_before | none_after


def weight_kernel(nz, rx, tiles, own_map, pa, la, got_one, got_two, own_side, wc, maps, ppe, ppo, lbe, lbo):
    we, wo, ce, co = (wc.at[k] for k in range(4))
    wide = rx + 2 * HALO
    groups = wide // 4
    clear_pads((ppe, ppo), wide, nz)
    row, column = grid_of(128, 256)
    cell = cell_of(place_of(column))
    own = ones_where(row == cell)
    row, column = grid_of(32, 256)
    cell = cell_of(place_of(column))
    low_side = cell < 0
    from_low, from_high = cell + HALO, cell - 128
    pot_low = ones_where(
        low_side & (((row < HALO) & (row == from_low)) | (between(row, 12, 16) & (row == from_low + 4)))
    )
    pot_high = ones_where(
        (cell >= 128) & (((row < HALO) & (row == from_high)) | (between(row, 12, 16) & (row == from_high + 12)))
    )
    lab_low = ones_where(low_side & between(row, 16, 28) & (row == from_low + 16))
    lab_high = ones_where((cell >= 128) & between(row, 16, 28) & (row == from_high + 16))

    def moved(matrix, q):
        pieces = [jnp.zeros((32, 256), bf16)] * 4
        pieces[q] = matrix
        return jnp.concatenate(pieces, axis=0)

    flat = (groups * nz, 128)
    even = is_even("gy")
    swapped_one = got_one[pl.ds(0, groups)].reshape(flat)
    swapped_two = got_two[pl.ds(0, groups)].reshape(flat)
    left = jnp.where(even, swapped_two, swapped_one)
    right = jnp.where(even, swapped_one, swapped_two)
    for q in range(4):
        value = pa[pl.ds(q, groups, stride=4)].reshape(flat)
        high, middle, low = parts_of(value)
        pot = product(jnp.concatenate([high, left], axis=1), jnp.concatenate([own, moved(pot_low, q)], axis=0))
        pot = pot + product(
            jnp.concatenate([middle, right], axis=1), jnp.concatenate([own, moved(pot_high, q)], axis=0)
        )
        pot = (pot + product(low, own)).reshape(groups, nz, 256)
        ppe[pl.ds(q, groups, stride=4), pl.ds(8, nz), :] = pot[:, :, :128]
        ppo[pl.ds(q, groups, stride=4), pl.ds(8, nz), :] = pot[:, :, 128:]
        code = la[pl.ds(q, groups, stride=4)].reshape(flat).astype(bf16)
        lab = product(jnp.concatenate([code, left], axis=1), jnp.concatenate([own, moved(lab_low, q)], axis=0))
        lab = (lab + product(right, moved(lab_high, q))).reshape(groups, nz, 256)
        lbe[pl.ds(q, groups, stride=4)] = lab[:, :, :128]
        lbo[pl.ds(q, groups, stride=4)] = lab[:, :, 128:]
    lane = lane_iota(nz)
    kept = []
    for t in (0, 1):
        place = 2 * lane + t
        keep = (place < 136) | between(place, 149, 168) | between(place, 184, 203) | (place >= 248)
        kept.append(keep & ~absent(place))
    v0 = jnp.broadcast_to(own_map[pl.ds(16, 1), :], (nz, 128))
    v1 = jnp.broadcast_to(own_map[pl.ds(17, 1), :], (nz, 128))

    def rows(first, size):
        for k in range(size):
            i = first + k
            near = neighbour_rows((ppe, ppo), i, nz, read_row((ppe, ppo), i - 1, nz), read_row((ppe, ppo), i + 1, nz))
            for t, (p_ref, code_ref, w_out, c_out) in enumerate(((ppe, lbe, we, ce), (ppo, lbo, wo, co))):
                p = read(p_ref, i, nz)
                code = jnp.where(kept[t], code_ref[i], 0.0)
                growth = jnp.exp(p)
                inverse = 1.0 / (6.0 + debye_term * growth)
                plasma = between(code, 0.5, 1.5)
                edge = jnp.where(code < 2.5, v0, v1)
                w = jnp.where(plasma, (near[t] - 6.0 * p - debye_term * growth) * inverse, edge - p)
                w_out[i] = jnp.where(code > 0.5, w, 0.0)
                c_out[i] = jnp.where(plasma, inverse, 0.0)

    chunked(1, wide - 1, 86, rows)
    zero = jnp.zeros((nz, 128), f32)
    for i in (0, wide - 1):
        for ref in (we, wo, ce, co):
            ref[i] = zero
    map_one, map_two = got_one[groups].astype(f32)[0:8], got_two[groups].astype(f32)[0:8]
    all_maps = (jnp.where(even, map_two, map_one), own_side[groups].astype(f32)[0:8], jnp.where(even, map_one, map_two))
    per_plane = rx // (8 * tiles)
    tall = rx + TALL
    row = lax.broadcasted_iota(jnp.int32, (8, 128), 0)
    for k, index in enumerate(all_maps):
        z = jnp.floor((index + 0.5) / per_plane)
        part = index - z * per_plane
        depth = jnp.where(row == 2, part, per_plane - 1 - part)
        beside = jnp.where(depth * (8 * tiles) < HALO, z, float(nz)) * tall
        depth = jnp.where(depth * (8 * tiles) < HALO, depth, 0.0) * 8
        inner = z * tall + 16 + part * (8 * tiles)
        target = jnp.where(row == 1, inner, jnp.where(row == 0, beside + 8 - depth, beside + 16 + rx + depth))
        maps[pl.ds(8 * k, 8), :] = target.astype(jnp.int32)


def slot_kernel(count, ny, tiles, blocks_in, owners_in, volts_in, pot_in, lab_in, slots, own, pot, lab, *scratch):
    field, blocks, out, owners, volts, in_sems, out_sems = scratch
    rows = tiles * 8
    pairs = [(owners_in, owners), (volts_in, volts), (pot_in, pot), (lab_in, lab)]
    copies = [pltpu.make_async_copy(*pair, in_sems.at[4 + k]) for k, pair in enumerate(pairs)]
    width = rows * 128 // 4
    columns = [pl.ds(k * width, width) for k in range(4)]
    block_copies = [
        pltpu.make_async_copy(blocks_in.at[:, part], blocks.at[:, part], in_sems.at[k]) for k, part in enumerate(columns)
    ]
    for copy in block_copies + copies:
        copy.start()
    own[...] = jnp.zeros(own.shape, f32)
    for r in range(rows):
        if r % (rows // 4) == 0:
            block_copies[r // (rows // 4)].wait()
        field[pl.ds(r, count, stride=rows + 8), :] = blocks[:, pl.ds(r * 128, 128)].astype(f32)
    lane = lane_iota(8)
    sub = lax.broadcasted_iota(jnp.int32, (8, 128), 0)

    def one(k, carry):
        def tile(offset, t):
            brick = lax.rem(k + offset + count, count)
            return field[pl.ds(pl.multiple_of(brick * (rows + 8) + t * 8, 8), 8), :]

        parts = [tile(0, t) for t in range(tiles)]
        if tiles == 1:
            parts += [tile(ny, 0), tile(-ny, 0)]
        else:
            mixed = jnp.where(sub < 4, tile(ny, 1), tile(-ny, tiles - 2))
            parts += [tile(ny, 0), mixed, tile(-ny, tiles - 1)]

        def pair(offset, t, at):
            return roll(jnp.where(lane < 64, tile(offset + 1, t), tile(offset - 1, t)), HALO + at)

        sides = jnp.zeros((8, 128), f32)
        for t in range(tiles):
            sides = jnp.where(between(lane, 32 * t, 32 * t + 32), pair(0, t, 32 * t), sides)
        corners = jnp.where(lane < 32, pair(ny, 0, 0), pair(-ny, tiles - 1, 32))
        if tiles > 1:
            second = jnp.where(lane < 96, pair(ny, 1, 64), pair(-ny, tiles - 2, 96))
            corners = jnp.where(lane < 64, corners, second)
        parts += [sides, corners]
        out[k] = jnp.concatenate(parts, axis=0).astype(bf16)
        return carry

    part = count // 4
    out_copies = []
    for step in range(4):
        chunked(step * part, (step + 1) * part, 8, lambda first, size: [one(first + k, 0) for k in range(size)])
        span = pl.ds(step * part, part)
        out_copies.append(pltpu.make_async_copy(out.at[span], slots.at[span], out_sems.at[step]))
        out_copies[-1].start()
    for copy in copies:
        copy.wait()
    own[pl.ds(0, 16), pl.ds(0, count)] = jnp.broadcast_to(owners[...].astype(f32), (16, count))
    for k in (0, 1):
        own[pl.ds(16 + k, 1), :] = jnp.full((1, 128), volts[k], f32)
    for copy in out_copies:
        copy.wait()


def sweep_kernel(nz, rx, count, tiles, maps_in, got_in, wc, pot, out_hbm, *scratch):
    (re, ro, xe, xo, ye, yo, ue, uo, cut_e, cut_o, ch_a, ch_s, ve, vo, maps, got, out, map_sem, sems, out_sems) = scratch
    map_copy = pltpu.make_async_copy(maps_in, maps, map_sem)
    map_copy.start()
    some = count // 4
    got_copies = []
    for k in range(4):
        span = pl.ds(k * some, some)
        got_copies.append(pltpu.make_async_copy(got_in.at[span], got.at[span], sems.at[k]))
        got_copies[k].start()
    we, wo, ce, co = (wc.at[k] for k in range(4))
    rhs, xs, ys, us, cuts = (re, ro), (xe, xo), (ye, yo), (ue, uo), (cut_e, cut_o)
    weights, charged, couplings = (we, wo), (ve, vo), (ce, co)
    wide = rx + 2 * HALO
    tall = rx + TALL
    lane = lane_iota(nz)
    index_x, index_y = lax.axis_index("gx"), lax.axis_index("gy")
    low_x, high_x = index_x > 0, index_x < lax.axis_size("gx") - 1
    has_low, has_high = jnp.where(low_x, 1.0, 0.0), jnp.where(high_x, 1.0, 0.0)
    clear_pads(rhs + xs + ys + us, wide, nz)
    clear_pads(cuts, cut_e.shape[0], nz)

    low_lanes, high_lanes = lane_iota(8) < HALO, lane_iota(8) >= HALO

    def place(p):
        slot = got[p].astype(f32)
        pieces = [slot[8 * t : 8 * t + 8] for t in range(slot.shape[0] // 8)]

        def put(ref, row, value, mask=None):
            target = pl.ds(pl.multiple_of(row, 8), 8)
            if mask is None:
                ref[target, :] = value
            else:
                pltpu.store(ref.at[target, :], value, mask=mask)

        first = maps[9, p]
        for t in range(tiles):
            put(ch_a, first + t * 8, pieces[t])
        after, before = maps[10, p], maps[8, p]
        put(ch_a, after, pieces[tiles])
        if tiles == 1:
            put(ch_a, before, pieces[2])
        else:
            put(ch_a, after + 8, pieces[tiles + 1])
            put(ch_a, before - 8, pieces[tiles + 1])
            put(ch_a, before, pieces[tiles + 2])
        sides, corners = pieces[-2:]
        low_side, high_side = maps[1, p], maps[17, p]
        for t in range(tiles):
            value = roll(sides, -32 * t)
            put(ch_s, low_side + t * 8, value, low_lanes)
            put(ch_s, high_side + t * 8, value, high_lanes)
        for at, step in ((0, 1), (32, -1)):
            value = roll(corners, -at)
            second = None if tiles == 1 else roll(corners, -at - 64)
            for which, lanes in ((1 + step, low_lanes), (17 + step, high_lanes)):
                target = maps[which, p]
                put(ch_s, target, value, lanes)
                if tiles > 1:
                    put(ch_s, target + 8 * step, second, lanes)

    row, column = grid_of(256, 256)
    cell = cell_of(place_of(column))
    spread = ones_where(
        ((row < 128) & (row == cell))
        | (between(row, 128, 128 + HALO) & (row - (128 + HALO) == cell))
        | (between(row, 128 + HALO, 128 + 2 * HALO) & (row - HALO == cell))
    )
    source = cell_of(place_of(row))
    gather = jnp.where((source == cell) & (cell != NOWHERE), damping, 0.0).astype(bf16)
    row, column = grid_of(256, 128)
    final = ones_where(cell_of(place_of(row)) == column)
    is_strip = (lane < HALO) & (index_y > 0)
    is_strip = is_strip | (between(lane, HALO, 2 * HALO) & (index_y < lax.axis_size("gy") - 1))

    map_copy.wait()
    for k in range(4):
        got_copies[k].wait()
        chunked(k * some, (k + 1) * some, 8, lambda first, size: [place(first + p) for p in range(size)])

    def add_charge(present):
        def rows(first, size):
            both = []
            for k in range(size):
                x = first + k + 4
                a = ch_a[pl.ds(x, nz, stride=tall), :]
                strip = jnp.where(is_strip, ch_s[pl.ds(x, nz, stride=tall), :], 0.0)
                if present is not None:
                    a = jnp.where(present, a, 0.0)
                    strip = jnp.where(present, strip, 0.0)
                both.append(jnp.concatenate([a, strip], axis=1).astype(bf16))
            charge = product(jnp.concatenate(both, axis=0), spread)
            for k in range(size):
                i = first + k
                for t in (0, 1):
                    part = charge[k * nz : (k + 1) * nz, 128 * t : 128 * t + 128]
                    value = weights[t][i] + debye_term * couplings[t][i] * part
                    charged[t][i] = value
                    rhs[t][i, pl.ds(8, nz), :] = value

        return rows

    chunked(1, HALO, HALO, add_charge(low_x))
    chunked(HALO, HALO + rx, 64, add_charge(None))
    chunked(HALO + rx, wide - 1, HALO, add_charge(high_x))

    def iterate(src, dst, low, high):
        def rows(first, size):
            for k in range(size):
                i = first + k
                near = neighbour_rows(src, i, nz, read_row(src, i - 1, nz), read_row(src, i + 1, nz))
                for t in (0, 1):
                    dst[t][i, pl.ds(8, nz), :] = read(rhs[t], i, nz) + couplings[t][i] * near[t]

        chunked(low, high, 84, rows)

    def cut(level, at, edge, step):
        starts = {2: 0, 3: 1, 4: 3}
        whole = {2: rhs, 3: xs, 4: ys}[level]
        for j in range(level - 1):
            i = edge + step * j
            before = at + starts.get(level - 1, 0)
            changed = j < level - 2
            outer = None if j == 0 else read_row(cuts, before + j - 1, nz)
            inner = read_row(cuts, before + j + 1, nz) if j + 1 < level - 2 else read_row(whole, i + step, nz)
            near = neighbour_rows(cuts if changed else whole, before + j if changed else i, nz, outer, inner)
            for t in (0, 1):
                cuts[t][at + starts[level] + j, pl.ds(8, nz), :] = read(rhs[t], i, nz) + couplings[t][i] * near[t]

    ends = [(0, HALO + 7, -1), (6, HALO + rx - 8, 1), (12, HALO - 8, 1), (18, HALO + rx + 7, -1)]
    ghosts = [(2 * lane + t == 168) | (2 * lane + t == 183) | absent(2 * lane + t) for t in (0, 1)]
    own = lane < 64
    out_copies = []
    for sweep in range(3):
        last = sweep == 2
        lowest = 1 + 4 * sweep
        if sweep > 0:

            def residual(first, size):
                for k in range(size):
                    i = first + k
                    near = neighbour_rows(us, i, nz, read_row(us, i - 1, nz), read_row(us, i + 1, nz))
                    for t in (0, 1):
                        held = jnp.where(ghosts[t], 0.0, charged[t][i] - read(us[t], i, nz))
                        shared = jnp.where(ghosts[t], 0.0, near[t])
                        rhs[t][i, pl.ds(8, nz), :] = held + couplings[t][i] * shared

            chunked(lowest, wide - lowest, 84, residual)
        low, high = lowest + 3, wide - lowest - 3
        for level, src, dst in ((2, rhs, xs), (3, xs, ys), (4, ys, xs)):
            for at, edge, step in ends if sweep == 0 else ends[:2]:
                cut(level, at, edge, step)
            iterate(src, dst, lowest + level - 1, wide - lowest - level + 1)

        def scale(first, end, factor):
            for i in range(first, end):
                for t in (0, 1):
                    xs[t][i, pl.ds(8, nz), :] = read(xs[t], i, nz) * factor

        def add_cut(at, edge, step, factor, kept):
            for j in range(3):
                i = edge + step * j
                for t in (0, 1):
                    whole = read(xs[t], i, nz)
                    part = read(cuts[t], at + 3 + j, nz)
                    xs[t][i, pl.ds(8, nz), :] = (part + factor * whole) if kept else (whole + factor * part)

        mid_low, mid_high = HALO + 7, HALO + rx - 8
        if sweep == 0:
            add_cut(*ends[2], has_low, True)
            add_cut(*ends[3], has_high, True)
            scale(low + 3, mid_low - 2, 1.0 + has_low)
            scale(mid_high + 3, high - 3, 1.0 + has_high)
        else:
            scale(low, mid_low - 2, 1.0 + has_low)
            scale(mid_high + 3, high, 1.0 + has_high)
        add_cut(*ends[0], has_low, False)
        add_cut(*ends[1], has_high, False)

        def join(first, size):
            flat = (size * nz, 128)
            both = [xs[t][pl.ds(first, size), pl.ds(8, nz), :].reshape(flat) for t in (0, 1)]
            if last:
                keep = lane_iota(size * nz) < 64
                both = [
                    damping * both[t]
                    + jnp.where(keep, us[t][pl.ds(first, size), pl.ds(8, nz), :].reshape(flat), 0.0)
                    for t in (0, 1)
                ]
            whole = jnp.concatenate(both, axis=1)
            high = whole.astype(bf16)
            rest = (whole - high.astype(f32)).astype(bf16)
            matrix = final if last else gather
            total = product(rest, matrix) + product(high, matrix)
            if last:
                for k in range(size):
                    x = first + k - HALO
                    out[pl.ds(x, nz, stride=rx), :] = total[k * nz : (k + 1) * nz] + pot[pl.ds(x, nz, stride=rx), :]
                span = pl.ds(first - HALO, size)
                copy = pltpu.make_async_copy(
                    out.reshape(nz, rx, 128).at[:, span], out_hbm.at[:, span], out_sems.at[len(out_copies)]
                )
                copy.start()
                out_copies.append(copy)
                return
            for t in (0, 1):
                value = total[:, 128 * t : 128 * t + 128].reshape(size, nz, 128)
                if sweep > 0:
                    value = value + us[t][pl.ds(first, size), pl.ds(8, nz), :]
                us[t][pl.ds(first, size), pl.ds(8, nz), :] = value

        step = 32 if last else JOIN
        for first in range(low, high, step):
            join(first, min(step, high - first))
    for copy in out_copies:
        copy.wait()


def vmem():
    return pl.BlockSpec(memory_space=pltpu.VMEM)


def smem():
    return pl.BlockSpec(memory_space=pltpu.SMEM)


def hbm():
    return pl.BlockSpec(memory_space=pltpu.HBM)


def anywhere():
    return pl.BlockSpec(memory_space=pl.ANY)


def call(kernel, ins, outs, scratch=(), aliases=(), room=8):
    return pl.pallas_call(
        kernel,
        in_specs=ins,
        out_specs=jax.tree.map(lambda _: vmem(), outs),
        out_shape=outs,
        scratch_shapes=list(scratch),
        input_output_aliases=dict(aliases),
        compiler_params=pltpu.CompilerParams(vmem_limit_bytes=room << 20),
    )


def swapped(value, axis, first):
    pairs = []
    for low in range(first, lax.axis_size(axis) - 1, 2):
        pairs += [(low, low + 1), (low + 1, low)]
    return lax.ppermute(value, axis, pairs)


def on_device(potential, labels, voltages, ion_blocks, owner_map):
    nz, rx, ry = potential.shape
    wide = rx + 2 * HALO
    blocks = ion_blocks[0]
    count, cells = blocks.shape
    tiles = cells // (8 * ry)
    sds = jax.ShapeDtypeStruct
    ny = lax.axis_size("gy")

    slot_rows = 8 * (tiles + (2 if tiles == 1 else 3) + 2)
    slot_shape = (count, slot_rows, ry)
    brick = (nz, rx, ry)
    slots, own_map, potential, labels = pl.pallas_call(
        functools.partial(slot_kernel, count, ny, tiles),
        in_specs=[hbm()] * 5,
        out_specs=(hbm(), vmem(), vmem(), vmem()),
        out_shape=(sds(slot_shape, bf16), sds((24, ry), f32), sds(brick, f32), sds(brick, jnp.int32)),
        scratch_shapes=[
            pltpu.VMEM((count * (tiles + 1) * 8, 128), f32),
            pltpu.VMEM((count, cells), bf16),
            pltpu.VMEM(slot_shape, bf16),
            pltpu.VMEM((1, count), jnp.int32),
            pltpu.SMEM((2,), f32),
            pltpu.SemaphoreType.DMA((8,)),
            pltpu.SemaphoreType.DMA((4,)),
        ],
        compiler_params=pltpu.CompilerParams(vmem_limit_bytes=12 << 20),
    )(*(pltpu.with_memory_space_constraint(v, pltpu.HBM) for v in (blocks, owner_map.reshape(1, count), voltages, potential, labels)))
    pot = potential.reshape(nz * rx, ry)
    lab = labels.reshape(nz * rx, ry)

    strip = sds((2 * HALO + 5, nz, ry), bf16)
    one, two = call(
        functools.partial(x_pack_kernel, nz, rx),
        [vmem()] * 3,
        (strip, strip),
    )(pot, lab, own_map)
    one = swapped(one, "gx", 0)
    two = swapped(two, "gx", 1)

    got = lax.all_to_all(slots, ("gx", "gy"), split_axis=0, concat_axis=0, tiled=True)

    field = sds((wide, nz, ry), f32)
    side = sds((wide // 4 + 1, nz, ry), bf16)
    packed = (field, field, side, side)
    pa, la, left, right = call(functools.partial(y_own_kernel, nz, rx), [vmem()] * 2, packed)(pot, lab)
    pa, la, left, right = call(
        functools.partial(y_edge_kernel, nz, rx), [vmem()] * 7, packed, (), {3: 0, 4: 1, 5: 2, 6: 3}
    )(own_map, one, two, pa, la, left, right)
    got_one = swapped(left, "gy", 0)
    got_two = swapped(right, "gy", 1)
    padded = pltpu.VMEM((wide, nz + 16, 128), f32)
    wc, maps = call(
        functools.partial(weight_kernel, nz, rx, tiles),
        [vmem()] * 6,
        (sds((4, wide, nz, ry), f32), sds((24, 128), jnp.int32)),
        [padded, padded]
        + [pltpu.VMEM((wide, nz, 128), f32)] * 2,
        room=16,
    )(own_map, pa, la, got_one, got_two, left)
    cuts = pltpu.VMEM((24, nz + 16, 128), f32)
    plane = pltpu.VMEM(((nz + 1) * (rx + TALL), 128), f32)
    return pl.pallas_call(
        functools.partial(sweep_kernel, nz, rx, count, tiles),
        in_specs=[anywhere(), hbm(), vmem(), vmem()],
        out_specs=hbm(),
        out_shape=sds(brick, f32),
        scratch_shapes=[padded] * 8
        + [cuts, cuts]
        + [plane] * 2
        + [pltpu.VMEM((wide, nz, 128), f32)] * 2
        + [
            pltpu.SMEM((24, 128), jnp.int32),
            pltpu.VMEM(slot_shape, bf16),
            pltpu.VMEM((nz * rx, ry), f32),
            pltpu.SemaphoreType.DMA,
            pltpu.SemaphoreType.DMA((4,)),
            pltpu.SemaphoreType.DMA((-(-rx // 16),)),
        ],
        compiler_params=pltpu.CompilerParams(vmem_limit_bytes=24 << 20),
    )(maps, pltpu.with_memory_space_constraint(got, pltpu.HBM), wc, pot)


def solution(mesh):
    placed = (
        P(None, "gx", "gy"),
        P(None, "gx", "gy"),
        P(),
        P(("gx", "gy"), None, None),
        P(None, ("gx", "gy")),
    )
    return jax.shard_map(
        on_device, mesh=mesh, in_specs=placed, out_specs=P(None, "gx", "gy"), check_vma=False
    )
```
